32 devices in a mesh: dp: 8 (over z, x), segment: 2 (over y), mp: 2 (over core).
Axes of the slice: x: 2, y: 2, z: 4, core: 2. Of those that a mesh axis runs over, the one named last changes fastest.
Arguments:
- prefix_hidden: bfloat16 [16, 512, 8192], P(('dp', 'segment'), 'mp'), may hold values from -6 to 6
- norm_gain: float32 [8192], replicated, may hold values from 0.5 to 1.5
- kv_weight: bfloat16 [8192, 2, 1024], P('dp', None, 'mp'), may hold values from -0.0625 to 0.0625
- action_query: bfloat16 [16, 128, 2048], P(('dp', 'segment'), None, 'mp'), may hold values from -104 to 104
- action_kv: bfloat16 [16, 128, 2, 1024], P(('dp', 'segment'), None, None, 'mp'), may hold values from -4.25 to 4.25
- out_cotangent: bfloat16 [16, 128, 2048], P(('dp', 'segment'), None, 'mp'), may hold values from -18 to 18
- prefix_blocks: int32 [16, 512], P(('dp', 'segment')), may hold values from 0 to 7, as said below
- action_blocks: int32 [16, 128], P(('dp', 'segment')), may hold values from 0 to 8, as said below
- prefix_lengths: int32 [16], P(('dp', 'segment')), may hold values from 128 to 512, as said below
- timesteps: int32 [16], P(('dp', 'segment')), may hold values from 0 to 999
Outputs:
- attn_out: bfloat16 [16, 128, 2048], P(('dp', 'segment'), None, 'mp')
- query_grad: float32 [16, 128, 2048], P(('dp', 'segment'), None, 'mp')
- action_kv_grad: float32 [16, 128, 2, 1024], P(('dp', 'segment'), None, None, 'mp')
- weight_grad: float32 [8192, 2, 1024], P('dp', None, 'mp')
The draws below stay inside these ranges and needn't reach their ends.
Inputs may be any that keep to these rules, and one draw needn't show every extreme that they name: `prefix_blocks`: constant over each run of 64 positions, 0 on the first run, rising by 0 or 1 from one run to the next; in every draw some sample rises at every run. `action_blocks`: constant over each run of 64 positions; the last run of every sample holds 8; in every draw some sample's first run holds 0. `prefix_lengths`: in every draw some sample's prefix is whole and some sample's is 128.
All inputs are finite; a program needn't handle non-finite values.
Results may differ from the reference program's by a relative error of at most 0.017.
Values may be sent and summed in bfloat16 or wider, within the bound.
A program may use at most 128 MiB of HBM per device.

```python
import jax
import jax.numpy as jnp
from jax import lax

D = 8192
KVH = 8
HD = 128
QH = 16
PREFIX = 512
ACT = 128
TILE = 64
STEPS = 1000
SAMPLES = 16


def paired_actions(key):
    base = jax.random.fold_in(key, 31)
    pairs = jnp.clip(jax.random.normal(jax.random.fold_in(base, 1), (SAMPLES, ACT, 2, KVH * HD), jnp.float32), -4.0, 4.0)
    queries = jnp.clip(jax.random.normal(jax.random.fold_in(base, 2), (SAMPLES, ACT, QH * HD), jnp.float32), -4.0, 4.0)
    return (pairs, queries)


def draw_action_kv(key, part):
    return paired_actions(key)[0].astype(jnp.bfloat16)


def draw_action_query(key, part):
    return paired_actions(key)[1].astype(jnp.bfloat16)


def draw_prefix_blocks(key, part):
    tiles = PREFIX // TILE
    rises = jax.random.randint(jax.random.fold_in(key, 21), (SAMPLES, tiles), 0, 2)
    chosen = jax.random.randint(jax.random.fold_in(key, 25), (), 0, SAMPLES)
    rises = jnp.where((jnp.arange(SAMPLES) == chosen)[:, None], 1, rises)
    rises = rises.at[:, 0].set(0)
    levels = jnp.cumsum(rises, axis=1).astype(jnp.int32)
    return jnp.repeat(levels, TILE, axis=1).astype(jnp.int32)


def draw_action_blocks(key, part):
    tiles = ACT // TILE
    highest = PREFIX // TILE
    levels = jax.random.randint(jax.random.fold_in(key, 22), (SAMPLES, tiles), 0, highest + 1)
    chosen = jax.random.randint(jax.random.fold_in(key, 26), (), 0, SAMPLES)
    levels = levels.at[chosen, 0].set(0)
    levels = levels.at[:, tiles - 1].set(highest)
    return jnp.repeat(levels, TILE, axis=1).astype(jnp.int32)


def draw_prefix_lengths(key, part):
    lengths = jax.random.randint(jax.random.fold_in(key, 23), (SAMPLES,), PREFIX // 4, PREFIX + 1)
    chosen = jax.random.randint(jax.random.fold_in(key, 24), (), 0, SAMPLES)
    index = jnp.arange(SAMPLES)
    lengths = jnp.where(index == (chosen + 1) % SAMPLES, PREFIX // 4, lengths)
    return jnp.where(index == chosen, PREFIX, lengths).astype(jnp.int32)


def place_ends(entries, rng, smallest, largest):
    longest = entries.shape.index(max(entries.shape))
    spots = []
    for shift in (0, 1):
        where = [jax.random.randint(jax.random.fold_in(rng, axis), (), 0, length) for axis, length in enumerate(entries.shape)]
        where[longest] = (where[longest] + shift) % entries.shape[longest]
        spots.append(tuple(where))
    return entries.at[spots[0]].set(smallest).at[spots[1]].set(largest)


def spiked(result, stream_key, source, target, parts, factor):
    def block_of(axis_at):
        return (jnp.arange(result.shape[axis_at]) // (result.shape[axis_at] // parts)).reshape((-1,) + (1,) * (result.ndim - 1 - axis_at))

    near = jax.random.permutation(stream_key, parts)[block_of(target)]
    other_side = (block_of(target) + parts // 2) % parts
    return jnp.where((block_of(source) == near) | (block_of(source) == other_side), factor * result, result)


def shard_levels(own_key, extent, shards, least, largest):
    factor_of = 1.0
    for position, parts in shards:
        heights = jax.random.uniform(jax.random.fold_in(jax.random.fold_in(own_key, 6), position), (parts,), jnp.float32, least / len(shards), largest / len(shards))
        factor_of = factor_of * jnp.repeat(jnp.exp(heights), extent[position] // parts).reshape((-1,) + (1,) * (len(extent) - 1 - position))
    return factor_of


def centred(rng, extent, deviation, most, cuts=(), held_as=jnp.bfloat16):
    entries = deviation * jax.random.normal(rng, extent, jnp.float32)
    if cuts:
        entries = entries * shard_levels(rng, extent, cuts, -0.22, 0.18)
    return jnp.clip(entries, -most, most).astype(held_as)


def heavy_noise(key, shape, scale, limit, shards, heavy, kind=jnp.bfloat16):
    values = scale * jax.random.normal(key, shape, jnp.float32)
    if shards:
        values = values * shard_levels(key, shape, shards, -0.22, 0.18)
    return jnp.clip(spiked(values, jax.random.fold_in(key, 3), *heavy), -limit, limit).astype(kind)


def setup_inputs(seed: int = 0) -> dict:
    key_list = jax.random.split(jax.random.key(seed), 11)
    prefix_hidden = heavy_noise(key_list[0], (SAMPLES, PREFIX, D), 1.0, 6.0, ((0, 16), (1, 2)), (0, 2, 16, 2.0))
    norm_gain = jnp.clip(1.0 + 0.1 * jax.random.normal(key_list[1], (D,), jnp.float32), 0.5, 1.5)
    kv_weight = centred(key_list[2], (D, 2, KVH * HD), D ** -0.5, 0.0625, ((0, 8), (2, 2)))
    action_query = draw_action_query(jax.random.fold_in(key_list[10], 71), 0)
    action_kv = draw_action_kv(jax.random.fold_in(key_list[10], 71), 0)
    out_cotangent = centred(key_list[5], (SAMPLES, ACT, QH * HD), 3.0, 18.0, ((0, 16), (2, 2)))
    prefix_blocks = draw_prefix_blocks(jax.random.fold_in(key_list[10], 71), 0)
    action_blocks = draw_action_blocks(jax.random.fold_in(key_list[10], 71), 0)
    prefix_lengths = draw_prefix_lengths(jax.random.fold_in(key_list[10], 71), 0)
    timesteps = place_ends(jax.random.randint(key_list[9], (SAMPLES,), 0, STEPS), jax.random.fold_in(key_list[9], 1), 0, STEPS - 1).astype(jnp.int32)
    return dict(prefix_hidden=prefix_hidden, norm_gain=norm_gain, kv_weight=kv_weight, action_query=action_query, action_kv=action_kv, out_cotangent=out_cotangent, prefix_blocks=prefix_blocks, action_blocks=action_blocks, prefix_lengths=prefix_lengths, timesteps=timesteps)


EPS = 1e-06
NEGATIVE = -1e+30

def attention_pass(query, keys, values, visible, grad_out):
    scale = HD ** (-0.5)
    scores = jnp.einsum('agrh,jgh->graj', query.astype(jnp.float32), keys.astype(jnp.float32)) * scale
    masked = jnp.where(visible, scores, NEGATIVE)
    top = lax.optimization_barrier(jnp.max(masked, axis=-1, keepdims=True))
    expo = jnp.where(visible, jnp.exp(masked - top), 0.0)
    probs = expo / lax.optimization_barrier(jnp.sum(expo, axis=-1, keepdims=True))
    probs_low = lax.optimization_barrier(probs.astype(jnp.bfloat16)).astype(jnp.float32)
    out = jnp.einsum('graj,jgh->agrh', probs_low, values.astype(jnp.float32))
    d_probs = jnp.einsum('agrh,jgh->graj', grad_out.astype(jnp.float32), values.astype(jnp.float32))
    delta = lax.optimization_barrier(jnp.sum(probs * d_probs, axis=-1, keepdims=True))
    d_scores = lax.optimization_barrier((probs * (d_probs - delta)).astype(jnp.bfloat16)).astype(jnp.float32)
    d_query = jnp.einsum('graj,jgh->agrh', d_scores, keys.astype(jnp.float32)) * scale
    d_keys = jnp.einsum('graj,agrh->jgh', d_scores, query.astype(jnp.float32)) * scale
    d_values = jnp.einsum('graj,agrh->jgh', probs_low, grad_out.astype(jnp.float32))
    return (out, d_query, d_keys, d_values)

def reference(prefix_hidden, norm_gain, kv_weight, action_query, action_kv, out_cotangent, prefix_blocks, action_blocks, prefix_lengths, timesteps):
    ratio = QH // KVH
    columns = 2 * KVH * HD
    weight_flat = kv_weight.reshape(D, columns)
    positions = jnp.arange(PREFIX, dtype=jnp.int32)

    def one_sample(carry, inputs):
        hidden, query, own_pair, cotangent, pblocks, ablocks, length, level = inputs
        wide = hidden.astype(jnp.float32)
        inverse = lax.rsqrt(lax.optimization_barrier(jnp.mean(wide * wide, axis=-1, keepdims=True)) + EPS)
        normed = (wide * inverse * norm_gain).astype(jnp.bfloat16)
        prefix_kv = jnp.dot(normed, weight_flat, preferred_element_type=jnp.float32).astype(jnp.bfloat16)
        prefix_kv = prefix_kv.reshape(PREFIX, 2, KVH, HD)
        action_pair = own_pair.reshape(ACT, 2, KVH, HD)
        keys = jnp.concatenate([prefix_kv[:, 0], action_pair[:, 0]], axis=0)
        values = jnp.concatenate([prefix_kv[:, 1], action_pair[:, 1]], axis=0)
        see_prefix = (pblocks[None, :] <= ablocks[:, None]) & (positions[None, :] < length)
        see_action = ablocks[None, :] <= ablocks[:, None]
        visible = jnp.concatenate([see_prefix, see_action], axis=1)
        flow_weight = 0.5 + (level.astype(jnp.float32) + 0.5) / STEPS
        grad_out = (flow_weight * cotangent.astype(jnp.float32)).astype(jnp.bfloat16).reshape(ACT, KVH, ratio, HD)
        out, d_query, d_keys, d_values = attention_pass(query.reshape(ACT, KVH, ratio, HD), keys, values, visible, grad_out)
        d_pair = jnp.stack([d_keys, d_values], axis=1)
        prefix_grad = d_pair[:PREFIX].astype(jnp.bfloat16).reshape(PREFIX, columns)
        term = jnp.dot(normed.T, prefix_grad, preferred_element_type=jnp.float32)
        carry = carry + lax.optimization_barrier(term.astype(jnp.bfloat16)).astype(jnp.float32)
        results = (out.astype(jnp.bfloat16).reshape(ACT, QH * HD), d_query.reshape(ACT, QH * HD), d_pair[PREFIX:].reshape(ACT, 2, KVH * HD))
        return (carry, results)
    start = jnp.zeros((D, columns), jnp.float32)
    total, outputs = lax.scan(one_sample, start, (prefix_hidden, action_query, action_kv, out_cotangent, prefix_blocks, action_blocks, prefix_lengths, timesteps))
    attn_out, query_grad, action_kv_grad = outputs
    return (attn_out, query_grad, action_kv_grad, total.reshape(D, 2, KVH * HD))
```

```python
import functools

import jax
import jax.numpy as jnp
from jax import lax
from jax.experimental import pallas as pl
from jax.experimental.pallas import tpu as pltpu
from jax.sharding import PartitionSpec as P

HD = 128
QH = 16
KVH = 8
STEPS = 1000
EPS = 1e-06
NEGATIVE = -1e30
MiB = 1 << 20
PAIR = 2 * HD


def remote(src, dst, send_sem, recv_sem, where):
    return pltpu.make_async_remote_copy(
        src_ref=src,
        dst_ref=dst,
        send_sem=send_sem,
        recv_sem=recv_sem,
        device_id=where,
        device_id_type=pl.DeviceIdType.MESH,
    )


def first_axis(chunk):
    return 1 if chunk % 4 == 1 else 0


class Plan:
    def __init__(self, nz, chunks):
        self.nz, self.chunks = nz, chunks
        self.free = dict(core=0.0, x=0.0, s=0.0, z=0.0, m=0.0)
        self.arrived = {}
        self.pending = []
        self.order = []

    def add(self, key, needs, cost, sends, rank):
        self.pending.append((key, needs, cost, sends, rank))

    def run(self):
        done = set()
        while self.pending:
            best = None
            for entry in self.pending:
                key, needs, cost, sends, rank = entry
                if any(n not in self.arrived for n in needs):
                    continue
                ready = max([self.free["core"]] + [self.arrived[n] for n in needs])
                pick = (ready, rank)
                if best is None or pick < best[0]:
                    best = (pick, entry)
            (ready, _), entry = best
            self.pending.remove(entry)
            key, needs, cost, sends, rank = entry
            self.order.append(key)
            self.arrived[key] = ready + cost
            self.free["core"] = ready + cost
            for name, link, size in sends:
                start = max(ready + cost, self.free[link])
                self.free[link] = start + size
                self.arrived[name] = start + size + 1.5
        return self.order


UNIT = 5.6


def stages(nz, chunks):
    plan = Plan(nz, chunks)
    piece = UNIT
    for c in range(chunks):
        needs = [] if c < 2 else [("wf", c - 2, nz - 1)]
        plan.add(("wo", c), needs, 0.1, [(("w", c, 1), "z", piece)], c * 0.01)
        for k in range(1, nz):
            needs = [("w", c, k)] + ([("wf", c, k - 1)] if k > 1 else [("wo", c)])
            sends = [(("w", c, k + 1), "z", piece)] if k < nz - 1 else []
            plan.add(("wf", c, k), needs, 0.1, sends, 1)
    for j in range(nz):
        needs = [("ns", j - 1)] if j else [("wo", 0)]
        plan.add(
            ("ns", j), needs, 0.1,
            [(("nx", j), "x", piece), (("ny", j), "s", piece), (("nd", j), "x", piece), (("nd2", j), "s", piece)], 0.005,
        )
        plan.add(("nf", j), [("nx", j), ("ny", j), ("nd", j), ("nd2", j)], 0.1, [(("nm", j), "m", 2.0)], 2)
    for c in range(chunks):
        one, two = ("x", "s") if first_axis(c) == 0 else ("s", "x")
        needs = [("nm", j) for j in range(nz)] + [("wf", c, k) for k in range(1, nz)]
        plan.add(("A", c), needs, 3.0, [(("p", c), one, 2 * piece)], 10 + c)
        plan.add(("B", c), [("A", c), ("p", c)], 0.5, [(("y", c), two, piece)], 7)
        plan.add(
            ("C", c), [("B", c), ("y", c)], 2.0,
            [(("g0", c), two, piece), (("g1", c), one, piece)], 6,
        )
        plan.add(("G", c), [("C", c), ("g0", c)], 0.1, [(("g2", c), one, piece)], 4)
        plan.add(("D", c), [("G", c), ("g1", c), ("g2", c)] + ([("F", c - 2)] if c >= 2 else []), 3.3, [], 9)
        for off in range(nz - 1, 0, -1):
            needs = [("D", c)] if off == nz - 1 else [("E", c, off + 1), ("e", c, off + 1)]
            plan.add(("E", c, off), needs, 0.3, [(("e", c, off), "z", piece)], 3)
        plan.add(("F", c), [("E", c, 1), ("e", c, 1)], 0.3, [(("o", c), "s", piece)], 5)
    return plan.run()


def kernel(
    order, nz, nmp, ratio,
    w_ref, n_ref, q_ref, akv_ref, go_ref, vis_ref,
    out_ref, dq_ref, dakv_ref, o_ref,
    nb, wb, keep, ps, px, ys, yb, gb, dw, zs, zb,
    w_send, w_recv, own_n, own_w, n_send, n_recv, f_send, f_recv,
    p_send, p_recv, y_send, y_recv, g_send, g_recv, z_send, z_recv, o_send, o_recv,
):
    dp, seg, mp = lax.axis_index("dp"), lax.axis_index("segment"), lax.axis_index("mp")
    z, x = dp // 2, dp % 2
    chunks, half = w_ref.shape[0], w_ref.shape[1]
    tokens = n_ref.shape[0]
    samples, rows = nb.shape[0], nb.shape[1]
    others = nmp - 1
    acts = q_ref.shape[0]
    scale = HD ** (-0.5)

    x_dp = z * 2 + (1 - x)
    plane = [
        {"dp": x_dp},
        {"segment": 1 - seg},
        {"dp": x_dp, "segment": 1 - seg},
    ]
    plane_xs = [(1 - x, seg), (x, 1 - seg), (1 - x, 1 - seg)]
    m_peer = [{"mp": (mp + o) % nmp} for o in range(1, nmp)]
    up = {"dp": (z + 1) * 2 + x}
    down = {"dp": (z - 1) * 2 + x}
    has_up, has_down = z < nz - 1, z > 0
    mine = x * 2 + seg

    barrier = pltpu.get_barrier_semaphore()
    for peer in plane + m_peer:
        pl.semaphore_signal(barrier, inc=1, device_id=peer, device_id_type=pl.DeviceIdType.MESH)

    @pl.when(has_up)
    def _():
        pl.semaphore_signal(barrier, inc=1, device_id=up, device_id_type=pl.DeviceIdType.MESH)

    @pl.when(has_down)
    def _():
        pl.semaphore_signal(barrier, inc=1, device_id=down, device_id_type=pl.DeviceIdType.MESH)

    ends = has_up.astype(jnp.int32) + has_down.astype(jnp.int32)
    pl.semaphore_wait(barrier, len(plane) + len(m_peer) + ends)

    def block(b):
        return pl.ds(pl.multiple_of(b * half, half), half)

    def columns(b, to_x, to_s):
        return pl.ds(pl.multiple_of(((b * 2 + to_x) * 2 + to_s) * half, half), half)

    def rows_of(m):
        return pl.ds(pl.multiple_of(m * tokens, tokens), tokens)

    def dot(a, b, ca, cb):
        return lax.dot_general(a, b, (((ca,), (cb,)), ((), ())), preferred_element_type=jnp.float32)

    def w_copy(c, k, upward):
        src_block = z - k if upward else z + k
        src = w_ref.at[c] if k == 0 else wb.at[c, block(src_block)]
        return remote(
            src, wb.at[c, block(src_block)],
            w_send.at[int(upward), c, k], w_recv.at[c, src_block], up if upward else down,
        )

    def w_arrival(c, k, upward):
        src_block = z - k if upward else z + k
        part = wb.at[c, block(src_block)]
        return remote(part, part, w_send.at[int(upward), c, k], w_recv.at[c, src_block], down if upward else up)

    def w_keep(c):
        return pltpu.make_async_copy(w_ref.at[c], wb.at[c, block(z)], own_w.at[c])

    def weights_own(c):
        @pl.when(has_up)
        def _():
            w_copy(c, 0, True).start()

        @pl.when(has_down)
        def _():
            w_copy(c, 0, False).start()

        w_keep(c).start()

    def weights_forward(c, k):
        @pl.when(z - k >= 0)
        def _():
            w_arrival(c, k, True).wait_recv()
            if k < nz - 1:
                @pl.when(has_up)
                def _():
                    w_copy(c, k, True).start()

        @pl.when(z + k < nz)
        def _():
            w_arrival(c, k, False).wait_recv()
            if k < nz - 1:
                @pl.when(has_down)
                def _():
                    w_copy(c, k, False).start()

    def n_copy(p, j):
        to_x, to_s = plane_xs[p]
        return remote(
            n_ref.at[:, columns(j, to_x, to_s)], nb.at[mine, rows_of(mp), block(j)],
            n_send.at[p, j], n_recv.at[p, j], plane[p],
        )

    def n_keep(j):
        return pltpu.make_async_copy(
            n_ref.at[:, columns(j, x, seg)], nb.at[mine, rows_of(mp), block(j)], own_n.at[j]
        )

    def f_copy(p, j, o):
        if p == 3:
            return remote(
                n_ref.at[:, columns(j, x, seg)], nb.at[mine, rows_of(mp), block(j)],
                f_send.at[p, j, o], f_recv.at[p, j, o], m_peer[o],
            )
        from_x, from_s = plane_xs[p]
        part = nb.at[from_x * 2 + from_s, rows_of(mp), block(j)]
        return remote(part, part, f_send.at[p, j, o], f_recv.at[p, j, o], m_peer[o])

    def tokens_send(j):
        for p in (2, 0, 1):
            n_copy(p, j).start()
        n_keep(j).start()
        for o in range(others):
            f_copy(3, j, o).start()

    def tokens_forward(j):
        for p in range(3):
            n_copy(p, j).wait_recv()
            for o in range(others):
                f_copy(p, j, o).start()

    def tokens_wait():
        for j in range(nz):
            n_keep(j).wait()
            for p in range(4):
                for o in range(others):
                    f_copy(p, j, o).wait_recv()

    tile = min(rows, 512)

    def tiles(body):
        if rows == tile:
            body(pl.ds(0, tile))
        else:
            @pl.loop(0, rows // tile)
            def _(i):
                body(pl.ds(pl.multiple_of(i * tile, tile), tile))

    def sample(c, a, b):
        return a * 2 + b if first_axis(c) == 0 else b * 2 + a

    def coords(c):
        return (x, seg) if first_axis(c) == 0 else (seg, x)

    def peers(c):
        return (plane[0], plane[1]) if first_axis(c) == 0 else (plane[1], plane[0])

    def p_copy(c):
        return remote(ps.at[c], px.at[c], p_send.at[c], p_recv.at[c], peers(c)[0])

    def y_copy(c):
        return remote(ys.at[c], yb.at[c], y_send.at[c], y_recv.at[c], peers(c)[1])

    def partial_sums(c):
        if c == 0:
            tokens_wait()
        w_keep(c).wait()
        a, _ = coords(c)

        @pl.loop(0, 2)
        def _(b):
            q = sample(c, 1 - a, b)

            def body(part):
                ps[c, b, part, :] = dot(nb[q, part, :], wb[c], 1, 0).astype(jnp.bfloat16)

            tiles(body)

        p_copy(c).start()

        @pl.loop(0, 2)
        def _(b):
            q = sample(c, a, b)

            def body(part):
                keep[c, b, part, :] = dot(nb[q, part, :], wb[c], 1, 0)

            tiles(body)

    def second_sums(c):
        _, b = coords(c)
        p_copy(c).wait_recv()
        ys[c] = (keep[c, 1 - b] + px[c, 1 - b].astype(jnp.float32)).astype(jnp.bfloat16)
        y_copy(c).start()
        keep[c, b] = keep[c, b] + px[c, b].astype(jnp.float32)

    def g_copy(c, i):
        one, two = peers(c)
        a, b = coords(c)
        q = sample(c, a, 1 - b) if i == 2 else mine
        part = gb.at[c, q]
        return remote(part, part, g_send.at[c, i], g_recv.at[c, i], two if i == 0 else one)

    vis = vis_ref[...]
    visible = jnp.concatenate([vis] * ratio, axis=0) > 0.5

    def attend(c):
        _, b = coords(c)
        y_copy(c).wait_recv()
        pair = (keep[c, b] + yb[c].astype(jnp.float32)).astype(jnp.bfloat16)
        cols = slice(c * HD, (c + 1) * HD)
        keys = jnp.concatenate([pair[:, :HD], akv_ref[0, :, cols]], axis=0)
        values = jnp.concatenate([pair[:, HD:], akv_ref[1, :, cols]], axis=0)
        hs = [slice((c * ratio + r) * HD, (c * ratio + r + 1) * HD) for r in range(ratio)]
        query = jnp.concatenate([q_ref[:, h] for h in hs], axis=0)
        go = jnp.concatenate([go_ref[:, h] for h in hs], axis=0)
        masked = jnp.where(visible, dot(query, keys, 1, 1) * scale, NEGATIVE)
        top = jnp.max(masked, axis=-1, keepdims=True)
        expo = jnp.where(visible, jnp.exp(masked - top), 0.0)
        probs = expo * (1.0 / jnp.sum(expo, axis=-1, keepdims=True))
        low = probs.astype(jnp.bfloat16)
        d_probs = dot(go, values, 1, 1)
        delta = jnp.sum(probs * d_probs, axis=-1, keepdims=True)
        d_scores = (probs * (d_probs - delta)).astype(jnp.bfloat16)
        d_keys = dot(d_scores, query, 0, 0) * scale
        d_values = dot(low, go, 0, 0)
        gb[c, mine, :, :HD] = d_keys[:rows].astype(jnp.bfloat16)
        gb[c, mine, :, HD:] = d_values[:rows].astype(jnp.bfloat16)
        g_copy(c, 0).start()
        g_copy(c, 1).start()
        dakv_ref[0, :, cols] = d_keys[rows:]
        dakv_ref[1, :, cols] = d_values[rows:]
        out = dot(low, values, 1, 0).astype(jnp.bfloat16)
        d_query = dot(d_scores, keys, 1, 0) * scale
        for r, h in enumerate(hs):
            out_ref[:, h] = out[r * acts : (r + 1) * acts]
            dq_ref[:, h] = d_query[r * acts : (r + 1) * acts]

    def grads_forward(c):
        g_copy(c, 0).wait_recv()
        g_copy(c, 2).start()

    depth = min(nz * half, 512)

    def weight_terms(c):
        g_copy(c, 1).wait_recv()
        g_copy(c, 2).wait_recv()

        @pl.loop(0, nz * half // depth)
        def _(i):
            cols = pl.ds(pl.multiple_of(i * depth, depth), depth)
            total = dot(nb[0, :, cols], gb[c, 0], 0, 0)
            for q in range(1, samples):
                total = total + dot(nb[q, :, cols], gb[c, q], 0, 0)
            dw[c % 2, cols, :] = total

    def z_copy(c, off, upward):
        to = z + off if upward else z - off
        slot = nz if (not upward and off == 1) else to
        return remote(
            zs.at[c, to], zb.at[c, slot], z_send.at[c, to], z_recv.at[c, slot], up if upward else down
        )

    def z_arrival(c, slot, upward):
        part = zb.at[c, slot]
        return remote(part, part, z_send.at[c, z], z_recv.at[c, slot], down if upward else up)

    def chain(c, off):
        def step(to, upward):
            @pl.when(has_down if upward else has_up)
            def _():
                z_arrival(c, to, upward).wait_recv()

            zs[c, to] = (dw[c % 2, block(to), :] + zb[c, to].astype(jnp.float32)).astype(jnp.bfloat16)
            z_copy(c, off, upward).start()

        @pl.when(z + off < nz)
        def _():
            step(z + off, True)

        @pl.when(z - off >= 0)
        def _():
            step(z - off, False)

    def o_copy(c):
        return remote(o_ref.at[c, seg], o_ref.at[c, seg], o_send.at[c], o_recv.at[c], plane[1])

    def finish(c):
        @pl.when(has_down)
        def _():
            z_arrival(c, z, True).wait_recv()

        @pl.when(has_up)
        def _():
            z_arrival(c, nz, False).wait_recv()

        total = dw[c % 2, block(z), :] + zb[c, z].astype(jnp.float32) + zb[c, nz].astype(jnp.float32)
        o_ref[c, seg] = total.astype(jnp.bfloat16)
        o_copy(c).start()

    def clear():
        @pl.when(z == 0)
        def _():
            @pl.loop(0, chunks)
            def _(c):
                @pl.loop(0, nz)
                def _(b):
                    zb[c, b] = jnp.zeros(zb.shape[2:], zb.dtype)

        @pl.when(z == nz - 1)
        def _():
            @pl.loop(0, chunks)
            def _(c):
                @pl.loop(0, nz - 1)
                def _(b):
                    zb[c, b] = jnp.zeros(zb.shape[2:], zb.dtype)

                zb[c, nz] = jnp.zeros(zb.shape[2:], zb.dtype)

    bodies = dict(
        wo=weights_own, wf=weights_forward, ns=tokens_send, nf=tokens_forward,
        A=partial_sums, B=second_sums, C=attend, G=grads_forward, D=weight_terms, E=chain, F=finish,
    )
    cleared = False
    for stage in order:
        if stage[0] not in ("wo", "ns") and not cleared:
            clear()
            cleared = True
        bodies[stage[0]](*stage[1:])

    for c in range(chunks):
        o_copy(c).wait()
        p_copy(c).wait_send()
        y_copy(c).wait_send()
        for i in range(3):
            g_copy(c, i).wait_send()
        for off in range(nz - 1, 0, -1):
            @pl.when(z + off < nz)
            def _():
                z_copy(c, off, True).wait_send()

            @pl.when(z - off >= 0)
            def _():
                z_copy(c, off, False).wait_send()

        for k in range(nz - 1):
            @pl.when(jnp.logical_and(has_up, z - k >= 0))
            def _():
                w_copy(c, k, True).wait_send()

            @pl.when(jnp.logical_and(has_down, z + k < nz))
            def _():
                w_copy(c, k, False).wait_send()

    for j in range(nz):
        for p in range(3):
            n_copy(p, j).wait_send()
        for p in range(4):
            for o in range(others):
                f_copy(p, j, o).wait_send()


def fused(nz, nmp, ratio, weight, normed, query, akv, grad_out, visible):
    dma = pltpu.SemaphoreType.DMA
    vmem = pl.BlockSpec(memory_space=pltpu.VMEM)
    chunks, half, _ = weight.shape
    tokens = normed.shape[0]
    rows = nmp * tokens
    deep = nz * half
    acts, width = query.shape
    others = max(nmp - 1, 1)
    bf16, f32 = jnp.bfloat16, jnp.float32
    order = stages(nz, chunks)
    return pl.pallas_call(
        functools.partial(kernel, order, nz, nmp, ratio),
        out_shape=(
            jax.ShapeDtypeStruct((acts, width), bf16),
            jax.ShapeDtypeStruct((acts, width), f32),
            jax.ShapeDtypeStruct(akv.shape, f32),
            jax.ShapeDtypeStruct((chunks, 2, half, PAIR), bf16),
        ),
        in_specs=[vmem] * 6,
        out_specs=(vmem,) * 4,
        scratch_shapes=[
            pltpu.VMEM((4, rows, deep), bf16),
            pltpu.VMEM((chunks, deep, PAIR), bf16),
            pltpu.VMEM((chunks, 2, rows, PAIR), f32),
            pltpu.VMEM((chunks, 2, rows, PAIR), bf16),
            pltpu.VMEM((chunks, 2, rows, PAIR), bf16),
            pltpu.VMEM((chunks, rows, PAIR), bf16),
            pltpu.VMEM((chunks, rows, PAIR), bf16),
            pltpu.VMEM((chunks, 4, rows, PAIR), bf16),
            pltpu.VMEM((2, deep, PAIR), f32),
            pltpu.VMEM((chunks, nz, half, PAIR), bf16),
            pltpu.VMEM((chunks, nz + 1, half, PAIR), bf16),
            dma((2, chunks, nz)), dma((chunks, nz)), dma((nz,)), dma((chunks,)),
            dma((3, nz)), dma((3, nz)), dma((4, nz, others)), dma((4, nz, others)),
            dma((chunks,)), dma((chunks,)), dma((chunks,)), dma((chunks,)),
            dma((chunks, 3)), dma((chunks, 3)),
            dma((chunks, nz)), dma((chunks, nz + 1)),
            dma((chunks,)), dma((chunks,)),
        ],
        compiler_params=pltpu.CompilerParams(
            collective_id=0, has_side_effects=True, vmem_limit_bytes=60 * MiB
        ),
        name="fused",
    )(weight, normed, query, akv, grad_out, visible)


def shards(
    ndp,
    nmp,
    prefix_hidden,
    norm_gain,
    kv_weight,
    action_query,
    action_kv,
    out_cotangent,
    prefix_blocks,
    action_blocks,
    prefix_lengths,
    timesteps,
):
    nz = ndp // 2
    ratio = QH // KVH
    depth, _, columns = kv_weight.shape
    chunks = columns // HD
    half = depth // 2
    seg = lax.axis_index("segment")
    wide = prefix_hidden[0].astype(jnp.float32)
    inverse = lax.rsqrt(jnp.mean(wide * wide, axis=-1, keepdims=True) + EPS)
    normed_local = (wide * inverse * norm_gain).astype(jnp.bfloat16)
    own_weight = lax.dynamic_slice_in_dim(kv_weight, seg * half, half, axis=0)
    own_weight = own_weight.reshape(half, 2, chunks, HD).transpose(2, 0, 1, 3).reshape(chunks, half, PAIR)
    rows = nmp * normed_local.shape[0]
    flow_weight = 0.5 + (timesteps[0].astype(jnp.float32) + 0.5) / STEPS
    grad_out = (flow_weight * out_cotangent[0].astype(jnp.float32)).astype(jnp.bfloat16)
    pblocks = prefix_blocks[0]
    ablocks = action_blocks[0]
    positions = jnp.arange(rows, dtype=jnp.int32)
    see_prefix = (pblocks[None, :] <= ablocks[:, None]) & (positions[None, :] < prefix_lengths[0])
    see_action = ablocks[None, :] <= ablocks[:, None]
    visible = jnp.concatenate([see_prefix, see_action], axis=1).astype(jnp.float32)
    attn_out, query_grad, d_action, summed = fused(
        nz, nmp, ratio, own_weight, normed_local,
        action_query[0], action_kv[0].transpose(1, 0, 2), grad_out, visible,
    )
    weight_grad = summed.reshape(chunks, depth, 2, HD).transpose(1, 2, 0, 3).reshape(depth, 2, columns)
    return (
        attn_out[None],
        query_grad[None],
        d_action.transpose(1, 0, 2)[None],
        weight_grad.astype(jnp.float32),
    )


def solution(mesh):
    placed = (
        P(("dp", "segment"), "mp", None),
        P(),
        P("dp", None, "mp"),
        P(("dp", "segment"), None, "mp"),
        P(("dp", "segment"), None, None, "mp"),
        P(("dp", "segment"), None, "mp"),
        P(("dp", "segment"), None),
        P(("dp", "segment"), None),
        P(("dp", "segment")),
        P(("dp", "segment")),
    )
    return jax.shard_map(
        functools.partial(shards, mesh.shape["dp"], mesh.shape["mp"]),
        mesh=mesh,
        in_specs=placed,
        out_specs=(
            P(("dp", "segment"), None, "mp"),
            P(("dp", "segment"), None, "mp"),
            P(("dp", "segment"), None, None, "mp"),
            P("dp", None, "mp"),
        ),
        check_vma=False,
    )
```

```python
import functools

import jax
import jax.numpy as jnp
from jax import lax
from jax.experimental import pallas as pl
from jax.experimental.pallas import tpu as pltpu
from jax.sharding import PartitionSpec as P

HD = 128
QH = 16
KVH = 8
STEPS = 1000
EPS = 1e-06
NEGATIVE = -1e30
MiB = 1 << 20
PAIR = 2 * HD
KEPT = 3
STRIPS = 4
LIMIT = 45.5


def remote(src, dst, send_sem, recv_sem, where):
    return pltpu.make_async_remote_copy(
        src_ref=src,
        dst_ref=dst,
        send_sem=send_sem,
        recv_sem=recv_sem,
        device_id=where,
        device_id_type=pl.DeviceIdType.MESH,
    )


class Plan:
    def __init__(self, nz, chunks):
        self.nz, self.chunks = nz, chunks
        self.free = dict(core=0.0, x=0.0, s=0.0, z=0.0, m=0.0)
        self.arrived = {}
        self.pending = []
        self.order = []

    def add(self, key, needs, cost, sends, rank):
        self.pending.append((key, needs, cost, sends, rank))

    def run(self):
        done = set()
        while self.pending:
            best = None
            for entry in self.pending:
                key, needs, cost, sends, rank = entry
                if any(n not in self.arrived for n in needs):
                    continue
                ready = max([self.free["core"]] + [self.arrived[n] for n in needs])
                pick = (ready, rank)
                if best is None or pick < best[0]:
                    best = (pick, entry)
            (ready, _), entry = best
            self.pending.remove(entry)
            key, needs, cost, sends, rank = entry
            self.order.append(key)
            self.arrived[key] = ready + cost
            self.free["core"] = ready + cost
            for name, link, size in sends:
                start = max(ready + cost, self.free[link])
                self.free[link] = start + size
                self.arrived[name] = start + size + HOP
        return self.order


UNIT = 5.7
HOP = 1.7


FOUND = (
    ("ns", 0), ("ns", 1), ("wo", 0), ("ns", 2), ("wo", 1), ("wf", 0, 1), ("wf", 1, 1), ("wo", 2),
    ("wo", 3), ("ns", 3), ("wf", 2, 1), ("nf", 0), ("nf", 1), ("wf", 0, 2), ("nf", 2), ("wf", 1, 2),
    ("wf", 2, 2), ("nf", 3), ("wf", 0, 3), ("A", 0), ("B", 0, 1), ("wf", 1, 3), ("wf", 3, 1), ("B", 0, 0),
    ("A", 1), ("C", 0), ("wf", 2, 3), ("G", 0, 0), ("G", 0, 1), ("B", 1, 1), ("B", 1, 0), ("wf", 3, 2),
    ("A", 2), ("E", 0, 3), ("C", 1), ("E", 0, 2), ("G", 1, 1), ("E", 0, 1), ("G", 1, 0), ("B", 2, 1),
    ("wf", 3, 3), ("B", 2, 0), ("A", 3), ("E", 1, 3), ("E", 1, 2), ("C", 2), ("E", 1, 1), ("G", 2, 1),
    ("G", 2, 0), ("B", 3, 0), ("F", 0), ("B", 3, 1), ("E", 2, 3), ("E", 2, 2), ("C", 3), ("H", 0),
    ("E", 2, 1), ("G", 3, 0), ("G", 3, 1), ("F", 1), ("E", 3, 3), ("F", 2), ("E", 3, 2), ("H", 1),
    ("E", 3, 1), ("H", 2), ("F", 3), ("H", 3),
)


def stages(nz, chunks):
    made = modelled(nz, chunks)
    return list(FOUND) if set(FOUND) == set(made) else made


def modelled(nz, chunks):
    plan = Plan(nz, chunks)
    piece = UNIT
    for c in range(chunks):
        needs = [] if c < 2 else [("wf", c - 2, nz - 1)]
        plan.add(("wo", c), needs, 0.1, [(("w", c, 1), "z", piece)], c * 0.01)
        for k in range(1, nz):
            needs = [("w", c, k)] + ([("wf", c, k - 1)] if k > 1 else [("wo", c)])
            sends = [(("w", c, k + 1), "z", piece)] if k < nz - 1 else []
            plan.add(("wf", c, k), needs, 0.1, sends, 1)
    for j in range(STRIPS):
        needs = [("ns", j - 1)] if j else [("wo", 0)]
        plan.add(
            ("ns", j), needs, 0.1,
            [(("nx", j), "x", piece), (("ny", j), "s", piece), (("nd", j), "x", piece), (("nd2", j), "s", piece)], 0.005,
        )
        plan.add(("nf", j), [("nx", j), ("ny", j), ("nd", j), ("nd2", j)], 0.1, [(("nm", j), "m", 2.0)], 2)
    for c in range(chunks):
        needs = [("nm", j) for j in range(STRIPS)] + [("wf", c, k) for k in range(1, nz)]
        if c >= KEPT:
            needs.append(("C", c - KEPT))
        plan.add(("A", c), needs, 3.0, [(("p0", c), "x", piece), (("p1", c), "s", piece)], 10 + c)
        plan.add(("B", c, 0), [("A", c), ("p0", c)], 0.3, [(("y0", c), "s", piece / 2)], 7)
        plan.add(("B", c, 1), [("A", c), ("p1", c)], 0.3, [(("y1", c), "x", piece / 2)], 7)
        plan.add(
            ("C", c), [("B", c, 0), ("B", c, 1), ("y0", c), ("y1", c)], 2.5,
            [
                (("gx1", c), "x", piece / 2), (("gs0", c), "s", piece / 2),
                (("gx0", c), "x", piece / 2), (("gs1", c), "s", piece / 2),
            ], 6,
        )
        plan.add(("G", c, 0), [("C", c), ("gs0", c)], 0.1, [(("gf0", c), "x", piece / 2)], 4)
        plan.add(("G", c, 1), [("C", c), ("gx1", c)], 0.1, [(("gf1", c), "s", piece / 2)], 4)
        full = [("G", c, 0), ("G", c, 1), ("gx0", c), ("gs1", c), ("gf0", c), ("gf1", c)]
        for off in range(nz - 1, 0, -1):
            needs = full if off == nz - 1 else [("E", c, off + 1), ("e", c, off + 1)]
            plan.add(("E", c, off), needs, 1.2, [(("e", c, off), "z", piece)], 3)
        plan.add(("F", c), [("E", c, 1), ("e", c, 1)], 1.3, [(("o", c), "s", piece)], 5)
        plan.add(("H", c), [("F", c), ("o", c)], 0.5, [], 20)
    return plan.run()


def kernel(
    order, nz, nmp, ratio,
    w_hbm, h_hbm, gain_hbm, level_ref, length_ref, q_hbm, akv_hbm, cot_hbm, pb_hbm, ab_hbm,
    out_ref, dq_ref, dakv_ref, grad_ref,
    gain_ref, vis_ref, q_ref, akv_ref, cot_ref, pb_ref, ab_ref, w_raw, h_buf, n_ref, o_ref, nb, wb, keep, ps, px, ys, yb, gb, zs, zb,
    w_send, w_recv, own_n, load_w, load_h, load_more, n_send, n_recv, f_send, f_recv,
    p_send, p_recv, y_send, y_recv, g_send, g_recv, z_send, z_recv, o_send, o_recv,
):
    dp, seg, mp = lax.axis_index("dp"), lax.axis_index("segment"), lax.axis_index("mp")
    z, x = dp // 2, dp % 2
    chunks, half = wb.shape[0], w_raw.shape[0]
    tokens, features = h_hbm.shape
    strip = tokens // STRIPS
    samples, rows = nb.shape[0], nb.shape[1]
    others = nmp - 1
    acts = q_ref.shape[0]
    scale = HD ** (-0.5)

    x_dp = z * 2 + (1 - x)
    plane = [
        {"dp": x_dp},
        {"segment": 1 - seg},
        {"dp": x_dp, "segment": 1 - seg},
    ]
    plane_xs = [(1 - x, seg), (x, 1 - seg), (1 - x, 1 - seg)]
    m_peer = [{"mp": (mp + o) % nmp} for o in range(1, nmp)]
    up = {"dp": (z + 1) * 2 + x}
    down = {"dp": (z - 1) * 2 + x}
    has_up, has_down = z < nz - 1, z > 0
    mine = x * 2 + seg

    def h_load(j):
        return pltpu.make_async_copy(h_hbm.at[pl.ds(j * strip, strip)], h_buf.at[j % 2], load_h.at[j % 2])

    w_load = pltpu.make_async_copy(w_hbm.at[pl.ds(pl.multiple_of(seg * half, half), half)], w_raw, load_w.at[0])
    more = [
        pltpu.make_async_copy(src, dst, load_more.at[i])
        for i, (src, dst) in enumerate(
            [(gain_hbm, gain_ref), (q_hbm, q_ref), (akv_hbm, akv_ref), (cot_hbm, cot_ref), (pb_hbm, pb_ref), (ab_hbm, ab_ref)]
        )
    ]
    h_load(0).start()
    more[0].start()
    w_load.start()
    h_load(1).start()
    for copy in more[1:]:
        copy.start()

    barrier = pltpu.get_barrier_semaphore()
    for peer in plane + m_peer:
        pl.semaphore_signal(barrier, inc=1, device_id=peer, device_id_type=pl.DeviceIdType.MESH)

    @pl.when(has_up)
    def _():
        pl.semaphore_signal(barrier, inc=1, device_id=up, device_id_type=pl.DeviceIdType.MESH)

    @pl.when(has_down)
    def _():
        pl.semaphore_signal(barrier, inc=1, device_id=down, device_id_type=pl.DeviceIdType.MESH)

    ends = has_up.astype(jnp.int32) + has_down.astype(jnp.int32)
    pl.semaphore_wait(barrier, len(plane) + len(m_peer) + ends)

    def block(b):
        return pl.ds(pl.multiple_of(b * half, half), half)

    def rows_of(m, j):
        return pl.ds(pl.multiple_of(m * tokens + j * strip, strip), strip)

    def dot(a, b, ca, cb):
        return lax.dot_general(a, b, (((ca,), (cb,)), ((), ())), preferred_element_type=jnp.float32)

    def w_copy(c, k, upward):
        src_block = z - k if upward else z + k
        part = wb.at[c, block(src_block)]
        return remote(
            part, part,
            w_send.at[int(upward), c, k], w_recv.at[c, src_block], up if upward else down,
        )

    def w_arrival(c, k, upward):
        src_block = z - k if upward else z + k
        part = wb.at[c, block(src_block)]
        return remote(part, part, w_send.at[int(upward), c, k], w_recv.at[c, src_block], down if upward else up)

    def weights_own(c):
        if c == 0:
            w_load.wait()
        group = min(half, 128)

        @pl.loop(0, half // group)
        def _(i):
            first = pl.multiple_of(i * group, group)
            for kv in range(2):
                wb[c, pl.ds(pl.multiple_of(z * half + first, group), group), kv * HD : (kv + 1) * HD] = w_raw[
                    pl.ds(first, group), kv, c * HD : (c + 1) * HD
                ]

        @pl.when(has_up)
        def _():
            w_copy(c, 0, True).start()

        @pl.when(has_down)
        def _():
            w_copy(c, 0, False).start()

    def weights_forward(c, k):
        @pl.when(z - k >= 0)
        def _():
            w_arrival(c, k, True).wait_recv()
            if k < nz - 1:
                @pl.when(has_up)
                def _():
                    w_copy(c, k, True).start()

        @pl.when(z + k < nz)
        def _():
            w_arrival(c, k, False).wait_recv()
            if k < nz - 1:
                @pl.when(has_down)
                def _():
                    w_copy(c, k, False).start()

    plane_q = [a * 2 + b for a, b in plane_xs]

    def n_copy(p, j):
        return remote(
            n_ref.at[plane_q[p], pl.ds(j * strip, strip)], nb.at[mine, rows_of(mp, j)],
            n_send.at[p, j], n_recv.at[p, j], plane[p],
        )

    def n_keep(j):
        return pltpu.make_async_copy(
            n_ref.at[mine, pl.ds(j * strip, strip)], nb.at[mine, rows_of(mp, j)], own_n.at[j]
        )

    def f_copy(p, j, o):
        if p == 3:
            return remote(
                n_ref.at[mine, pl.ds(j * strip, strip)], nb.at[mine, rows_of(mp, j)],
                f_send.at[p, j, o], f_recv.at[p, j, o], m_peer[o],
            )
        part = nb.at[plane_q[p], rows_of(mp, j)]
        return remote(part, part, f_send.at[p, j, o], f_recv.at[p, j, o], m_peer[o])

    def normalize(j):
        h_load(j).wait()
        if j == 0:
            more[0].wait()
        group = min(strip, 16)
        wide = 1024 if features % 1024 == 0 else half

        @pl.loop(0, strip // group)
        def _(i):
            part = pl.ds(pl.multiple_of(i * group, group), group)
            into = pl.ds(pl.multiple_of(j * strip + i * group, group), group)
            total = jnp.zeros((group, 1), jnp.float32)
            for k in range(0, features, wide):
                piece = h_buf[j % 2, part, k : k + wide].astype(jnp.float32)
                total = total + jnp.sum(piece * piece, axis=-1, keepdims=True)
            inverse = lax.rsqrt(total / features + EPS)
            for b in range(nz):
                for q in range(4):
                    first = (b * 4 + q) * half
                    piece = h_buf[j % 2, part, first : first + half].astype(jnp.float32)
                    scaled = piece * inverse * gain_ref[:, first : first + half]
                    n_ref[q, into, b * half : (b + 1) * half] = scaled.astype(jnp.bfloat16)

        if j + 2 < STRIPS:
            h_load(j + 2).start()

    def tokens_send(j):
        normalize(j)
        for p in (2, 0, 1):
            n_copy(p, j).start()
        n_keep(j).start()
        for o in range(others):
            f_copy(3, j, o).start()

    def tokens_forward(j):
        for p in range(3):
            n_copy(p, j).wait_recv()
            for o in range(others):
                f_copy(p, j, o).start()

    def tokens_wait():
        for j in range(STRIPS):
            n_keep(j).wait()
            for p in range(4):
                for o in range(others):
                    f_copy(p, j, o).wait_recv()

    part_rows = rows // 2
    halves = [pl.ds(0, part_rows), pl.ds(part_rows, part_rows)]
    spot = [seg, x]

    def sample(h, first, second):
        return first * 2 + second if h == 0 else second * 2 + first

    def p_copy(c, h, i):
        b = spot[h] if i else 1 - spot[h]
        return remote(ps.at[c, h, b], px.at[c, h, b], p_send.at[c, h, i], p_recv.at[c, h, i], plane[h])

    def y_copy(c, h):
        return remote(ys.at[c, h], yb.at[c, h], y_send.at[c, h], y_recv.at[c, h], plane[1 - h])

    def partial_sums(c):
        if c == 0:
            tokens_wait()
        for i in range(2):
            for h in range(2):
                b = spot[h] if i else 1 - spot[h]
                q = sample(h, 1 - (x, seg)[h], b)
                ps[c, h, b] = dot(nb[q, halves[h], :], wb[c], 1, 0).astype(jnp.bfloat16)
                p_copy(c, h, i).start()
        for h in range(2):
            @pl.loop(0, 2)
            def _(b):
                q = sample(h, (x, seg)[h], b)
                keep[c % KEPT, h, b] = dot(nb[q, halves[h], :], wb[c], 1, 0)

    def second_sums(c, h):
        b = spot[h]
        p_copy(c, h, 0).wait_recv()
        ys[c, h] = (keep[c % KEPT, h, 1 - b] + px[c, h, 1 - b].astype(jnp.float32)).astype(jnp.bfloat16)
        y_copy(c, h).start()

    def g_copy(c, to, h):
        part = gb.at[c, mine, halves[h]]
        return remote(part, part, g_send.at[c, to, h], g_recv.at[c, to, h], plane[to])

    def g_forward(c, h):
        q = sample(h, (x, seg)[h], 1 - spot[h])
        part = gb.at[c, q, halves[h]]
        return remote(part, part, g_send.at[c, 2, h], g_recv.at[c, 2, h], plane[h])

    def visible_tokens():
        wide = jnp.broadcast_to(ab_ref[...].astype(jnp.float32), (acts, acts))
        levels = wide.T
        see_action = wide <= levels
        levels = jnp.concatenate([levels] * (rows // acts), axis=1)
        place = lax.broadcasted_iota(jnp.int32, (acts, rows), 1)
        see_prefix = (pb_ref[...].astype(jnp.float32) <= levels) & (place < length_ref[0])
        return jnp.concatenate([see_prefix.astype(jnp.float32), see_action.astype(jnp.float32)], axis=1)

    def attend(c):
        if c == 0:
            for copy in more[1:]:
                copy.wait()
            vis_ref[...] = visible_tokens()
        visible = jnp.concatenate([vis_ref[...]] * ratio, axis=0) > 0.5
        parts = []
        for h in range(2):
            y_copy(c, h).wait_recv()
            p_copy(c, h, 1).wait_recv()
            b = spot[h]
            parts.append(
                keep[c % KEPT, h, b] + px[c, h, b].astype(jnp.float32) + yb[c, h].astype(jnp.float32)
            )
        pair = jnp.concatenate(parts, axis=0).astype(jnp.bfloat16)
        cols = slice(c * HD, (c + 1) * HD)
        keys = jnp.concatenate([pair[:, :HD], akv_ref[:, 0, cols]], axis=0)
        values = jnp.concatenate([pair[:, HD:], akv_ref[:, 1, cols]], axis=0)
        hs = [slice((c * ratio + r) * HD, (c * ratio + r + 1) * HD) for r in range(ratio)]
        query = jnp.concatenate([q_ref[:, h] for h in hs], axis=0)
        cot = jnp.concatenate([cot_ref[:, h] for h in hs], axis=0)
        go = (level_ref[0] * cot.astype(jnp.float32)).astype(jnp.bfloat16)
        masked = jnp.where(visible, dot(query, keys, 1, 1) * scale, NEGATIVE)
        top = jnp.max(masked, axis=-1, keepdims=True)
        expo = jnp.where(visible, jnp.exp(masked - top), 0.0)
        probs = expo * (1.0 / jnp.sum(expo, axis=-1, keepdims=True))
        low = probs.astype(jnp.bfloat16)
        d_probs = dot(go, values, 1, 1)
        delta = jnp.sum(probs * d_probs, axis=-1, keepdims=True)
        d_scores = (probs * (d_probs - delta)).astype(jnp.bfloat16)
        d_keys = dot(d_scores, query, 0, 0) * scale
        d_values = dot(low, go, 0, 0)
        gb[c, mine, :, :HD] = d_keys[:rows].astype(jnp.bfloat16)
        gb[c, mine, :, HD:] = d_values[:rows].astype(jnp.bfloat16)
        for h in range(2):
            g_copy(c, 0, 1 - h).start()
            g_copy(c, 1, h).start()
        dakv_ref[:, 0, cols] = d_keys[rows:]
        dakv_ref[:, 1, cols] = d_values[rows:]
        out = dot(low, values, 1, 0).astype(jnp.bfloat16)
        d_query = dot(d_scores, keys, 1, 0) * scale
        for r, h in enumerate(hs):
            out_ref[:, h] = out[r * acts : (r + 1) * acts]
            dq_ref[:, h] = d_query[r * acts : (r + 1) * acts]

    def grads_forward(c, h):
        g_copy(c, 1 - h, h).wait_recv()
        g_forward(c, h).start()

    def grads_wait(c):
        for h in range(2):
            g_copy(c, h, h).wait_recv()
            g_forward(c, h).wait_recv()

    cuts = 2 if half % 256 == 0 else 1
    depth = half // cuts

    def weight_term(c, b, i):
        cols = pl.ds(pl.multiple_of(b * half + i * depth, depth), depth)
        total = dot(nb[0, :, cols], gb[c, 0], 0, 0)
        for q in range(1, samples):
            total = total + dot(nb[q, :, cols], gb[c, q], 0, 0)
        return total

    def half_of(i):
        return pl.ds(pl.multiple_of(i * depth, depth), depth)

    def z_copy(c, off, upward, i):
        to = z + off if upward else z - off
        slot = nz if (not upward and off == 1) else to
        return remote(
            zs.at[c, to, half_of(i)], zb.at[c, slot, half_of(i)],
            z_send.at[c, to, i], z_recv.at[c, slot, i], up if upward else down,
        )

    def z_arrival(c, slot, upward, i):
        part = zb.at[c, slot, half_of(i)]
        return remote(part, part, z_send.at[c, z, i], z_recv.at[c, slot, i], down if upward else up)

    def chain(c, off):
        if off == nz - 1:
            grads_wait(c)

        def step(to, upward):
            @pl.loop(0, cuts)
            def _(i):
                total = weight_term(c, to, i)

                @pl.when(has_down if upward else has_up)
                def _():
                    z_arrival(c, to, upward, i).wait_recv()

                zs[c, to, half_of(i), :] = (total + zb[c, to, half_of(i), :].astype(jnp.float32)).astype(jnp.bfloat16)
                z_copy(c, off, upward, i).start()

        @pl.when(z + off < nz)
        def _():
            step(z + off, True)

        @pl.when(z - off >= 0)
        def _():
            step(z - off, False)

    def o_copy(c, i):
        return remote(
            zs.at[c, z, half_of(i)], o_ref.at[c, half_of(i)], o_send.at[c, i], o_recv.at[c, i], plane[1]
        )

    def finish(c):
        @pl.loop(0, cuts)
        def _(i):
            part = half_of(i)
            total = weight_term(c, z, i)

            @pl.when(has_down)
            def _():
                z_arrival(c, z, True, i).wait_recv()

            @pl.when(has_up)
            def _():
                z_arrival(c, nz, False, i).wait_recv()

            total = total + zb[c, z, part, :].astype(jnp.float32) + zb[c, nz, part, :].astype(jnp.float32)
            zs[c, z, part, :] = total.astype(jnp.bfloat16)
            o_copy(c, i).start()

        spread(c, seg, zs.at[c, z])

    def spread(c, which, src):
        for i in range(2):
            first = which * (half * 2 * chunks) + c * 2 + i
            part = pl.ds(first, half, stride=2 * chunks)
            grad_ref[part, :] = src[:, i * HD : (i + 1) * HD].astype(jnp.float32)

    def other_half(c):
        for i in range(cuts):
            o_copy(c, i).wait()
        spread(c, 1 - seg, o_ref.at[c])

    def clear():
        @pl.when(z == 0)
        def _():
            @pl.loop(0, chunks)
            def _(c):
                @pl.loop(0, nz)
                def _(b):
                    zb[c, b] = jnp.zeros(zb.shape[2:], zb.dtype)

        @pl.when(z == nz - 1)
        def _():
            @pl.loop(0, chunks)
            def _(c):
                @pl.loop(0, nz - 1)
                def _(b):
                    zb[c, b] = jnp.zeros(zb.shape[2:], zb.dtype)

                zb[c, nz] = jnp.zeros(zb.shape[2:], zb.dtype)

    bodies = dict(
        wo=weights_own, wf=weights_forward, ns=tokens_send, nf=tokens_forward,
        A=partial_sums, B=second_sums, C=attend, G=grads_forward, E=chain, F=finish, H=other_half,
    )
    cleared = False
    for stage in order:
        if stage[0] not in ("wo", "ns") and not cleared:
            clear()
            cleared = True
        bodies[stage[0]](*stage[1:])

    for c in range(chunks):
        for h in range(2):
            p_copy(c, h, 0).wait_send()
            p_copy(c, h, 1).wait_send()
            y_copy(c, h).wait_send()
            for to in range(2):
                g_copy(c, to, h).wait_send()
            g_forward(c, h).wait_send()
        for off in range(nz - 1, 0, -1):
            @pl.when(z + off < nz)
            def _():
                for i in range(cuts):
                    z_copy(c, off, True, i).wait_send()

            @pl.when(z - off >= 0)
            def _():
                for i in range(cuts):
                    z_copy(c, off, False, i).wait_send()

        for k in range(nz - 1):
            @pl.when(jnp.logical_and(has_up, z - k >= 0))
            def _():
                w_copy(c, k, True).wait_send()

            @pl.when(jnp.logical_and(has_down, z + k < nz))
            def _():
                w_copy(c, k, False).wait_send()

    for j in range(STRIPS):
        for p in range(3):
            n_copy(p, j).wait_send()
        for p in range(4):
            for o in range(others):
                f_copy(p, j, o).wait_send()


def stay(array):
    return pltpu.with_memory_space_constraint(array, pltpu.HBM)


def fused(nz, nmp, ratio, weight, hidden, gain, level, length, query, akv, cotangent, pblocks, ablocks):
    dma = pltpu.SemaphoreType.DMA
    vmem = pl.BlockSpec(memory_space=pltpu.VMEM)
    smem = pl.BlockSpec(memory_space=pltpu.SMEM)
    anywhere = pl.BlockSpec(memory_space=pltpu.HBM)
    half, chunks = weight.shape[0] // 2, weight.shape[2] // HD
    tokens, features = hidden.shape
    rows = nmp * tokens
    deep = nz * half
    acts, width = query.shape
    others = max(nmp - 1, 1)
    bf16, f32 = jnp.bfloat16, jnp.float32
    order = stages(nz, chunks)
    return pl.pallas_call(
        functools.partial(kernel, order, nz, nmp, ratio),
        out_shape=(
            jax.ShapeDtypeStruct((acts, width), bf16),
            jax.ShapeDtypeStruct((acts, width), f32),
            jax.ShapeDtypeStruct(akv.shape, f32),
            jax.ShapeDtypeStruct((2 * half * chunks * 2, HD), f32),
        ),
        in_specs=[anywhere] * 3 + [smem] * 2 + [anywhere] * 5,
        out_specs=(vmem,) * 4,
        scratch_shapes=[
            pltpu.VMEM(gain.shape, f32),
            pltpu.VMEM((acts, rows + acts), f32),
            pltpu.VMEM(query.shape, bf16),
            pltpu.VMEM(akv.shape, bf16),
            pltpu.VMEM(cotangent.shape, bf16),
            pltpu.VMEM(pblocks.shape, jnp.int32),
            pltpu.VMEM(ablocks.shape, jnp.int32),
            pltpu.VMEM((half,) + weight.shape[1:], bf16),
            pltpu.VMEM((2, tokens // STRIPS, features), bf16),
            pltpu.VMEM((4, tokens, deep), bf16),
            pltpu.VMEM((chunks, half, PAIR), bf16),
            pltpu.VMEM((4, rows, deep), bf16),
            pltpu.VMEM((chunks, deep, PAIR), bf16),
            pltpu.VMEM((min(chunks, KEPT), 2, 2, rows // 2, PAIR), f32),
            pltpu.VMEM((chunks, 2, 2, rows // 2, PAIR), bf16),
            pltpu.VMEM((chunks, 2, 2, rows // 2, PAIR), bf16),
            pltpu.VMEM((chunks, 2, rows // 2, PAIR), bf16),
            pltpu.VMEM((chunks, 2, rows // 2, PAIR), bf16),
            pltpu.VMEM((chunks, 4, rows, PAIR), bf16),
            pltpu.VMEM((chunks, nz, half, PAIR), bf16),
            pltpu.VMEM((chunks, nz + 1, half, PAIR), bf16),
            dma((2, chunks, nz)), dma((chunks, nz)), dma((STRIPS,)), dma((1,)), dma((2,)), dma((6,)),
            dma((3, STRIPS)), dma((3, STRIPS)), dma((4, STRIPS, others)), dma((4, STRIPS, others)),
            dma((chunks, 2, 2)), dma((chunks, 2, 2)), dma((chunks, 2)), dma((chunks, 2)),
            dma((chunks, 3, 2)), dma((chunks, 3, 2)),
            dma((chunks, nz, 2)), dma((chunks, nz + 1, 2)),
            dma((chunks, 2)), dma((chunks, 2)),
        ],
        compiler_params=pltpu.CompilerParams(
            collective_id=0, has_side_effects=True, vmem_limit_bytes=int(LIMIT * MiB)
        ),
        name="fused",
    )(
        *[stay(a) for a in (weight, hidden, gain)],
        level,
        length,
        *[stay(a) for a in (query, akv, cotangent, pblocks, ablocks)],
    )


def shards(
    ndp,
    nmp,
    prefix_hidden,
    norm_gain,
    kv_weight,
    action_query,
    action_kv,
    out_cotangent,
    prefix_blocks,
    action_blocks,
    prefix_lengths,
    timesteps,
):
    nz = ndp // 2
    ratio = QH // KVH
    depth, _, columns = kv_weight.shape
    chunks = columns // HD
    level = 0.5 + (timesteps.astype(jnp.float32) + 0.5) / STEPS
    attn_out, query_grad, d_action, summed = fused(
        nz, nmp, ratio, kv_weight, prefix_hidden[0], norm_gain[None], level, prefix_lengths,
        action_query[0], action_kv[0], out_cotangent[0], prefix_blocks, action_blocks,
    )
    weight_grad = summed.reshape(depth, chunks, 2, HD).transpose(0, 2, 1, 3).reshape(depth, 2, columns)
    return (
        attn_out[None],
        query_grad[None],
        d_action[None],
        weight_grad,
    )


def solution(mesh):
    placed = (
        P(("dp", "segment"), "mp", None),
        P(),
        P("dp", None, "mp"),
        P(("dp", "segment"), None, "mp"),
        P(("dp", "segment"), None, None, "mp"),
        P(("dp", "segment"), None, "mp"),
        P(("dp", "segment"), None),
        P(("dp", "segment"), None),
        P(("dp", "segment")),
        P(("dp", "segment")),
    )
    return jax.shard_map(
        functools.partial(shards, mesh.shape["dp"], mesh.shape["mp"]),
        mesh=mesh,
        in_specs=placed,
        out_specs=(
            P(("dp", "segment"), None, "mp"),
            P(("dp", "segment"), None, "mp"),
            P(("dp", "segment"), None, None, "mp"),
            P("dp", None, "mp"),
        ),
        check_vma=False,
    )
```

```python
import functools

import jax
import jax.numpy as jnp
from jax import lax
from jax.experimental import pallas as pl
from jax.experimental.pallas import tpu as pltpu
from jax.sharding import PartitionSpec as P

HD = 128
QH = 16
KVH = 8
STEPS = 1000
EPS = 1e-06
NEGATIVE = -1e30
MiB = 1 << 20
PAIR = 2 * HD
KEPT = 3
CUTS = 4
STRIPS = 8
LIMIT = 45.5


def remote(src, dst, send_sem, recv_sem, where):
    return pltpu.make_async_remote_copy(
        src_ref=src,
        dst_ref=dst,
        send_sem=send_sem,
        recv_sem=recv_sem,
        device_id=where,
        device_id_type=pl.DeviceIdType.MESH,
    )


class Plan:
    def __init__(self, nz, chunks):
        self.nz, self.chunks = nz, chunks
        self.free = dict(core=0.0, x=0.0, s=0.0, z=0.0, m=0.0)
        self.arrived = {}
        self.pending = []
        self.order = []

    def add(self, key, needs, cost, sends, rank):
        self.pending.append((key, needs, cost, sends, rank))

    def run(self):
        done = set()
        while self.pending:
            best = None
            for entry in self.pending:
                key, needs, cost, sends, rank = entry
                if any(n not in self.arrived for n in needs):
                    continue
                ready = max([self.free["core"]] + [self.arrived[n] for n in needs])
                pick = (ready, rank)
                if best is None or pick < best[0]:
                    best = (pick, entry)
            (ready, _), entry = best
            self.pending.remove(entry)
            key, needs, cost, sends, rank = entry
            self.order.append(key)
            self.arrived[key] = ready + cost
            self.free["core"] = ready + cost
            for name, link, size in sends:
                start = max(ready + cost, self.free[link])
                self.free[link] = start + size
                self.arrived[name] = start + size + HOP
        return self.order


UNIT = 5.7
HOP = 1.7


FOUND = (
    ("ns", 0), ("wo", 0), ("ns", 1), ("ns", 2), ("ns", 3), ("ns", 4), ("ns", 5), ("wo", 1),
    ("wf", 0, 1), ("wf", 1, 1), ("wo", 2), ("wo", 3), ("ns", 6), ("ns", 7), ("wf", 2, 1), ("nf", 0),
    ("nf", 1), ("nf", 2), ("nf", 3), ("wf", 0, 2), ("nf", 4), ("nf", 5), ("wf", 1, 2), ("wf", 2, 2),
    ("nf", 6), ("nf", 7), ("wf", 0, 3), ("A", 0), ("B", 0, 1), ("wf", 1, 3), ("wf", 3, 1), ("B", 0, 0),
    ("A", 1), ("C", 0), ("wf", 2, 3), ("G", 0, 0), ("G", 0, 1), ("B", 1, 1), ("B", 1, 0), ("wf", 3, 2),
    ("A", 2), ("E", 0, 3), ("C", 1), ("E", 0, 2), ("G", 1, 1), ("E", 0, 1), ("G", 1, 0), ("B", 2, 1),
    ("wf", 3, 3), ("B", 2, 0), ("A", 3), ("E", 1, 3), ("E", 1, 2), ("C", 2), ("E", 1, 1), ("G", 2, 1),
    ("G", 2, 0), ("B", 3, 0), ("F", 0), ("B", 3, 1), ("E", 2, 3), ("E", 2, 2), ("C", 3), ("H", 0),
    ("E", 2, 1), ("G", 3, 0), ("G", 3, 1), ("F", 1), ("E", 3, 3), ("F", 2), ("E", 3, 2), ("H", 1),
    ("E", 3, 1), ("H", 2), ("F", 3), ("H", 3),
)


def stages(nz, chunks):
    made = modelled(nz, chunks)
    return list(FOUND) if set(FOUND) == set(made) else made


def modelled(nz, chunks):
    plan = Plan(nz, chunks)
    piece = UNIT
    for c in range(chunks):
        needs = [] if c < 2 else [("wf", c - 2, nz - 1)]
        plan.add(("wo", c), needs, 0.1, [(("w", c, 1), "z", piece)], c * 0.01)
        for k in range(1, nz):
            needs = [("w", c, k)] + ([("wf", c, k - 1)] if k > 1 else [("wo", c)])
            sends = [(("w", c, k + 1), "z", piece)] if k < nz - 1 else []
            plan.add(("wf", c, k), needs, 0.1, sends, 1)
    for j in range(STRIPS):
        needs = [("ns", j - 1)] if j else [("wo", 0)]
        plan.add(
            ("ns", j), needs, 0.1,
            [(("nx", j), "x", piece), (("ny", j), "s", piece), (("nd", j), "x", piece), (("nd2", j), "s", piece)], 0.005,
        )
        plan.add(("nf", j), [("nx", j), ("ny", j), ("nd", j), ("nd2", j)], 0.1, [(("nm", j), "m", 2.0)], 2)
    for c in range(chunks):
        needs = [("nm", j) for j in range(STRIPS)] + [("wf", c, k) for k in range(1, nz)]
        if c >= KEPT:
            needs.append(("C", c - KEPT))
        plan.add(("A", c), needs, 3.0, [(("p0", c), "x", piece), (("p1", c), "s", piece)], 10 + c)
        plan.add(("B", c, 0), [("A", c), ("p0", c)], 0.3, [(("y0", c), "s", piece / 2)], 7)
        plan.add(("B", c, 1), [("A", c), ("p1", c)], 0.3, [(("y1", c), "x", piece / 2)], 7)
        plan.add(
            ("C", c), [("B", c, 0), ("B", c, 1), ("y0", c), ("y1", c)], 2.5,
            [
                (("gx1", c), "x", piece / 2), (("gs0", c), "s", piece / 2),
                (("gx0", c), "x", piece / 2), (("gs1", c), "s", piece / 2),
            ], 6,
        )
        plan.add(("G", c, 0), [("C", c), ("gs0", c)], 0.1, [(("gf0", c), "x", piece / 2)], 4)
        plan.add(("G", c, 1), [("C", c), ("gx1", c)], 0.1, [(("gf1", c), "s", piece / 2)], 4)
        full = [("G", c, 0), ("G", c, 1), ("gx0", c), ("gs1", c), ("gf0", c), ("gf1", c)]
        for off in range(nz - 1, 0, -1):
            needs = full if off == nz - 1 else [("E", c, off + 1), ("e", c, off + 1)]
            plan.add(("E", c, off), needs, 1.2, [(("e", c, off), "z", piece)], 3)
        plan.add(("F", c), [("E", c, 1), ("e", c, 1)], 1.3, [(("o", c), "s", piece)], 5)
        plan.add(("H", c), [("F", c), ("o", c)], 0.5, [], 20)
    return plan.run()


def kernel(
    order, nz, nmp, ratio,
    w_hbm, h_hbm, gain_hbm, level_ref, length_ref, q_hbm, akv_hbm, cot_hbm, pb_hbm, ab_hbm,
    out_ref, dq_ref, dakv_ref, grad_ref,
    gain_ref, vis_ref, q_ref, akv_ref, cot_ref, pb_ref, ab_ref, w_raw, h_buf, n_ref, o_ref, nb, wb, keep, ps, px, ys, yb, gb, zs, zb,
    w_send, w_recv, own_n, load_w, load_h, load_more, n_send, n_recv, f_send, f_recv,
    p_send, p_recv, y_send, y_recv, g_send, g_recv, z_send, z_recv, o_send, o_recv,
):
    dp, seg, mp = lax.axis_index("dp"), lax.axis_index("segment"), lax.axis_index("mp")
    z, x = dp // 2, dp % 2
    chunks, half = wb.shape[0], w_raw.shape[0]
    tokens, features = h_hbm.shape
    strip = tokens // STRIPS
    samples, rows = nb.shape[0], nb.shape[1]
    others = nmp - 1
    acts = q_ref.shape[0]
    scale = HD ** (-0.5)

    x_dp = z * 2 + (1 - x)
    plane = [
        {"dp": x_dp},
        {"segment": 1 - seg},
        {"dp": x_dp, "segment": 1 - seg},
    ]
    plane_xs = [(1 - x, seg), (x, 1 - seg), (1 - x, 1 - seg)]
    m_peer = [{"mp": (mp + o) % nmp} for o in range(1, nmp)]
    up = {"dp": (z + 1) * 2 + x}
    down = {"dp": (z - 1) * 2 + x}
    has_up, has_down = z < nz - 1, z > 0
    mine = x * 2 + seg

    def h_load(j):
        return pltpu.make_async_copy(h_hbm.at[pl.ds(j * strip, strip)], h_buf.at[j % 2], load_h.at[j % 2])

    w_load = pltpu.make_async_copy(w_hbm.at[pl.ds(pl.multiple_of(seg * half, half), half)], w_raw, load_w.at[0])
    more = [
        pltpu.make_async_copy(src, dst, load_more.at[i])
        for i, (src, dst) in enumerate(
            [(gain_hbm, gain_ref), (q_hbm, q_ref), (akv_hbm, akv_ref), (cot_hbm, cot_ref), (pb_hbm, pb_ref), (ab_hbm, ab_ref)]
        )
    ]
    h_load(0).start()
    more[0].start()
    w_load.start()
    h_load(1).start()
    for copy in more[1:]:
        copy.start()

    barrier = pltpu.get_barrier_semaphore()
    for peer in plane + m_peer:
        pl.semaphore_signal(barrier, inc=1, device_id=peer, device_id_type=pl.DeviceIdType.MESH)

    @pl.when(has_up)
    def _():
        pl.semaphore_signal(barrier, inc=1, device_id=up, device_id_type=pl.DeviceIdType.MESH)

    @pl.when(has_down)
    def _():
        pl.semaphore_signal(barrier, inc=1, device_id=down, device_id_type=pl.DeviceIdType.MESH)

    ends = has_up.astype(jnp.int32) + has_down.astype(jnp.int32)
    pl.semaphore_wait(barrier, len(plane) + len(m_peer) + ends)

    def block(b):
        return pl.ds(pl.multiple_of(b * half, half), half)

    def rows_of(m, j):
        return pl.ds(pl.multiple_of(m * tokens + j * strip, strip), strip)

    def dot(a, b, ca, cb):
        return lax.dot_general(a, b, (((ca,), (cb,)), ((), ())), preferred_element_type=jnp.float32)

    def w_copy(c, k, upward):
        src_block = z - k if upward else z + k
        part = wb.at[c, block(src_block)]
        return remote(
            part, part,
            w_send.at[int(upward), c, k], w_recv.at[c, src_block], up if upward else down,
        )

    def w_arrival(c, k, upward):
        src_block = z - k if upward else z + k
        part = wb.at[c, block(src_block)]
        return remote(part, part, w_send.at[int(upward), c, k], w_recv.at[c, src_block], down if upward else up)

    def weights_own(c):
        if c == 0:
            w_load.wait()
        group = min(half, 128)

        @pl.loop(0, half // group)
        def _(i):
            first = pl.multiple_of(i * group, group)
            for kv in range(2):
                wb[c, pl.ds(pl.multiple_of(z * half + first, group), group), kv * HD : (kv + 1) * HD] = w_raw[
                    pl.ds(first, group), kv, c * HD : (c + 1) * HD
                ]

        @pl.when(has_up)
        def _():
            w_copy(c, 0, True).start()

        @pl.when(has_down)
        def _():
            w_copy(c, 0, False).start()

    def weights_forward(c, k):
        @pl.when(z - k >= 0)
        def _():
            w_arrival(c, k, True).wait_recv()
            if k < nz - 1:
                @pl.when(has_up)
                def _():
                    w_copy(c, k, True).start()

        @pl.when(z + k < nz)
        def _():
            w_arrival(c, k, False).wait_recv()
            if k < nz - 1:
                @pl.when(has_down)
                def _():
                    w_copy(c, k, False).start()

    plane_q = [a * 2 + b for a, b in plane_xs]

    def n_copy(p, j):
        return remote(
            n_ref.at[plane_q[p], pl.ds(j * strip, strip)], nb.at[mine, rows_of(mp, j)],
            n_send.at[p, j], n_recv.at[p, j], plane[p],
        )

    def n_keep(j):
        return pltpu.make_async_copy(
            n_ref.at[mine, pl.ds(j * strip, strip)], nb.at[mine, rows_of(mp, j)], own_n.at[j]
        )

    def f_copy(p, j, o):
        if p == 3:
            return remote(
                n_ref.at[mine, pl.ds(j * strip, strip)], nb.at[mine, rows_of(mp, j)],
                f_send.at[p, j, o], f_recv.at[p, j, o], m_peer[o],
            )
        part = nb.at[plane_q[p], rows_of(mp, j)]
        return remote(part, part, f_send.at[p, j, o], f_recv.at[p, j, o], m_peer[o])

    def normalize(j):
        h_load(j).wait()
        if j == 0:
            more[0].wait()
        group = min(strip, 16)
        wide = 1024 if features % 1024 == 0 else half

        @pl.loop(0, strip // group)
        def _(i):
            part = pl.ds(pl.multiple_of(i * group, group), group)
            into = pl.ds(pl.multiple_of(j * strip + i * group, group), group)
            total = jnp.zeros((group, 1), jnp.float32)
            for k in range(0, features, wide):
                piece = h_buf[j % 2, part, k : k + wide].astype(jnp.float32)
                total = total + jnp.sum(piece * piece, axis=-1, keepdims=True)
            inverse = lax.rsqrt(total / features + EPS)
            for b in range(nz):
                for q in range(4):
                    first = (b * 4 + q) * half
                    piece = h_buf[j % 2, part, first : first + half].astype(jnp.float32)
                    scaled = piece * inverse * gain_ref[:, first : first + half]
                    n_ref[q, into, b * half : (b + 1) * half] = scaled.astype(jnp.bfloat16)

        if j + 2 < STRIPS:
            h_load(j + 2).start()

    def tokens_send(j):
        normalize(j)
        for p in (2, 0, 1):
            n_copy(p, j).start()
        n_keep(j).start()
        for o in range(others):
            f_copy(3, j, o).start()

    def tokens_forward(j):
        for p in range(3):
            n_copy(p, j).wait_recv()
            for o in range(others):
                f_copy(p, j, o).start()

    def tokens_wait():
        for j in range(STRIPS):
            n_keep(j).wait()
            for p in range(4):
                for o in range(others):
                    f_copy(p, j, o).wait_recv()

    part_rows = rows // 2
    halves = [pl.ds(0, part_rows), pl.ds(part_rows, part_rows)]
    spot = [seg, x]

    def sample(h, first, second):
        return first * 2 + second if h == 0 else second * 2 + first

    def p_copy(c, h, i):
        b = spot[h] if i else 1 - spot[h]
        return remote(ps.at[c, h, b], px.at[c, h, b], p_send.at[c, h, i], p_recv.at[c, h, i], plane[h])

    def y_copy(c, h):
        return remote(ys.at[c, h], yb.at[c, h], y_send.at[c, h], y_recv.at[c, h], plane[1 - h])

    def partial_sums(c):
        if c == 0:
            tokens_wait()
        for i in range(2):
            for h in range(2):
                b = spot[h] if i else 1 - spot[h]
                q = sample(h, 1 - (x, seg)[h], b)
                ps[c, h, b] = dot(nb[q, halves[h], :], wb[c], 1, 0).astype(jnp.bfloat16)
                p_copy(c, h, i).start()
        for h in range(2):
            @pl.loop(0, 2)
            def _(b):
                q = sample(h, (x, seg)[h], b)
                keep[c % KEPT, h, b] = dot(nb[q, halves[h], :], wb[c], 1, 0)

    def second_sums(c, h):
        b = spot[h]
        p_copy(c, h, 0).wait_recv()
        ys[c, h] = (keep[c % KEPT, h, 1 - b] + px[c, h, 1 - b].astype(jnp.float32)).astype(jnp.bfloat16)
        y_copy(c, h).start()

    def g_copy(c, to, h):
        part = gb.at[c, mine, halves[h]]
        return remote(part, part, g_send.at[c, to, h], g_recv.at[c, to, h], plane[to])

    def g_forward(c, h):
        q = sample(h, (x, seg)[h], 1 - spot[h])
        part = gb.at[c, q, halves[h]]
        return remote(part, part, g_send.at[c, 2, h], g_recv.at[c, 2, h], plane[h])

    def visible_tokens():
        wide = jnp.broadcast_to(ab_ref[...].astype(jnp.float32), (acts, acts))
        levels = wide.T
        see_action = wide <= levels
        levels = jnp.concatenate([levels] * (rows // acts), axis=1)
        place = lax.broadcasted_iota(jnp.int32, (acts, rows), 1)
        see_prefix = (pb_ref[...].astype(jnp.float32) <= levels) & (place < length_ref[0])
        return jnp.concatenate([see_prefix.astype(jnp.float32), see_action.astype(jnp.float32)], axis=1)

    def attend(c):
        if c == 0:
            for copy in more[1:]:
                copy.wait()
            vis_ref[...] = visible_tokens()
        visible = jnp.concatenate([vis_ref[...]] * ratio, axis=0) > 0.5
        parts = []
        for h in range(2):
            y_copy(c, h).wait_recv()
            p_copy(c, h, 1).wait_recv()
            b = spot[h]
            parts.append(
                keep[c % KEPT, h, b] + px[c, h, b].astype(jnp.float32) + yb[c, h].astype(jnp.float32)
            )
        pair = jnp.concatenate(parts, axis=0).astype(jnp.bfloat16)
        cols = slice(c * HD, (c + 1) * HD)
        keys = jnp.concatenate([pair[:, :HD], akv_ref[:, 0, cols]], axis=0)
        values = jnp.concatenate([pair[:, HD:], akv_ref[:, 1, cols]], axis=0)
        hs = [slice((c * ratio + r) * HD, (c * ratio + r + 1) * HD) for r in range(ratio)]
        query = jnp.concatenate([q_ref[:, h] for h in hs], axis=0)
        cot = jnp.concatenate([cot_ref[:, h] for h in hs], axis=0)
        go = (level_ref[0] * cot.astype(jnp.float32)).astype(jnp.bfloat16)
        masked = jnp.where(visible, dot(query, keys, 1, 1) * scale, NEGATIVE)
        top = jnp.max(masked, axis=-1, keepdims=True)
        expo = jnp.where(visible, jnp.exp(masked - top), 0.0)
        probs = expo * (1.0 / jnp.sum(expo, axis=-1, keepdims=True))
        low = probs.astype(jnp.bfloat16)
        d_probs = dot(go, values, 1, 1)
        delta = jnp.sum(probs * d_probs, axis=-1, keepdims=True)
        d_scores = (probs * (d_probs - delta)).astype(jnp.bfloat16)
        d_keys = dot(d_scores, query, 0, 0) * scale
        d_values = dot(low, go, 0, 0)
        gb[c, mine, :, :HD] = d_keys[:rows].astype(jnp.bfloat16)
        gb[c, mine, :, HD:] = d_values[:rows].astype(jnp.bfloat16)
        for h in range(2):
            g_copy(c, 0, 1 - h).start()
            g_copy(c, 1, h).start()
        dakv_ref[:, 0, cols] = d_keys[rows:]
        dakv_ref[:, 1, cols] = d_values[rows:]
        out = dot(low, values, 1, 0).astype(jnp.bfloat16)
        d_query = dot(d_scores, keys, 1, 0) * scale
        for r, h in enumerate(hs):
            out_ref[:, h] = out[r * acts : (r + 1) * acts]
            dq_ref[:, h] = d_query[r * acts : (r + 1) * acts]

    def grads_forward(c, h):
        g_copy(c, 1 - h, h).wait_recv()
        g_forward(c, h).start()

    def grads_wait(c):
        for h in range(2):
            g_copy(c, h, h).wait_recv()
            g_forward(c, h).wait_recv()

    cuts = next(n for n in (CUTS, 2, 1) if half % (n * 128) == 0)
    depth = half // cuts

    def weight_term(c, b, i):
        cols = pl.ds(pl.multiple_of(b * half + i * depth, depth), depth)
        total = dot(nb[0, :, cols], gb[c, 0], 0, 0)
        for q in range(1, samples):
            total = total + dot(nb[q, :, cols], gb[c, q], 0, 0)
        return total

    def half_of(i):
        return pl.ds(pl.multiple_of(i * depth, depth), depth)

    def z_copy(c, off, upward, i):
        to = z + off if upward else z - off
        slot = nz if (not upward and off == 1) else to
        return remote(
            zs.at[c, to, half_of(i)], zb.at[c, slot, half_of(i)],
            z_send.at[c, to, i], z_recv.at[c, slot, i], up if upward else down,
        )

    def z_arrival(c, slot, upward, i):
        part = zb.at[c, slot, half_of(i)]
        return remote(part, part, z_send.at[c, z, i], z_recv.at[c, slot, i], down if upward else up)

    def chain(c, off):
        if off == nz - 1:
            grads_wait(c)

        def step(to, upward):
            @pl.loop(0, cuts)
            def _(i):
                total = weight_term(c, to, i)

                @pl.when(has_down if upward else has_up)
                def _():
                    z_arrival(c, to, upward, i).wait_recv()

                zs[c, to, half_of(i), :] = (total + zb[c, to, half_of(i), :].astype(jnp.float32)).astype(jnp.bfloat16)
                z_copy(c, off, upward, i).start()

        @pl.when(z + off < nz)
        def _():
            step(z + off, True)

        @pl.when(z - off >= 0)
        def _():
            step(z - off, False)

    def o_copy(c, i):
        return remote(
            zs.at[c, z, half_of(i)], o_ref.at[c, half_of(i)], o_send.at[c, i], o_recv.at[c, i], plane[1]
        )

    def finish(c):
        @pl.loop(0, cuts)
        def _(i):
            part = half_of(i)
            total = weight_term(c, z, i)

            @pl.when(has_down)
            def _():
                z_arrival(c, z, True, i).wait_recv()

            @pl.when(has_up)
            def _():
                z_arrival(c, nz, False, i).wait_recv()

            total = total + zb[c, z, part, :].astype(jnp.float32) + zb[c, nz, part, :].astype(jnp.float32)
            zs[c, z, part, :] = total.astype(jnp.bfloat16)
            o_copy(c, i).start()

        spread(c, seg, zs.at[c, z])

    def spread(c, which, src):
        for i in range(2):
            first = which * (half * 2 * chunks) + c * 2 + i
            part = pl.ds(first, half, stride=2 * chunks)
            grad_ref[part, :] = src[:, i * HD : (i + 1) * HD].astype(jnp.float32)

    def other_half(c):
        for i in range(cuts):
            o_copy(c, i).wait()
        spread(c, 1 - seg, o_ref.at[c])

    def clear():
        @pl.when(z == 0)
        def _():
            @pl.loop(0, chunks)
            def _(c):
                @pl.loop(0, nz)
                def _(b):
                    zb[c, b] = jnp.zeros(zb.shape[2:], zb.dtype)

        @pl.when(z == nz - 1)
        def _():
            @pl.loop(0, chunks)
            def _(c):
                @pl.loop(0, nz - 1)
                def _(b):
                    zb[c, b] = jnp.zeros(zb.shape[2:], zb.dtype)

                zb[c, nz] = jnp.zeros(zb.shape[2:], zb.dtype)

    bodies = dict(
        wo=weights_own, wf=weights_forward, ns=tokens_send, nf=tokens_forward,
        A=partial_sums, B=second_sums, C=attend, G=grads_forward, E=chain, F=finish, H=other_half,
    )
    cleared = False
    for stage in order:
        if stage[0] not in ("wo", "ns") and not cleared:
            clear()
            cleared = True
        bodies[stage[0]](*stage[1:])

    for c in range(chunks):
        for h in range(2):
            p_copy(c, h, 0).wait_send()
            p_copy(c, h, 1).wait_send()
            y_copy(c, h).wait_send()
            for to in range(2):
                g_copy(c, to, h).wait_send()
            g_forward(c, h).wait_send()
        for off in range(nz - 1, 0, -1):
            @pl.when(z + off < nz)
            def _():
                for i in range(cuts):
                    z_copy(c, off, True, i).wait_send()

            @pl.when(z - off >= 0)
            def _():
                for i in range(cuts):
                    z_copy(c, off, False, i).wait_send()

        for k in range(nz - 1):
            @pl.when(jnp.logical_and(has_up, z - k >= 0))
            def _():
                w_copy(c, k, True).wait_send()

            @pl.when(jnp.logical_and(has_down, z + k < nz))
            def _():
                w_copy(c, k, False).wait_send()

    for j in range(STRIPS):
        for p in range(3):
            n_copy(p, j).wait_send()
        for p in range(4):
            for o in range(others):
                f_copy(p, j, o).wait_send()


def stay(array):
    return pltpu.with_memory_space_constraint(array, pltpu.HBM)


def fused(nz, nmp, ratio, weight, hidden, gain, level, length, query, akv, cotangent, pblocks, ablocks):
    dma = pltpu.SemaphoreType.DMA
    vmem = pl.BlockSpec(memory_space=pltpu.VMEM)
    smem = pl.BlockSpec(memory_space=pltpu.SMEM)
    anywhere = pl.BlockSpec(memory_space=pltpu.HBM)
    half, chunks = weight.shape[0] // 2, weight.shape[2] // HD
    tokens, features = hidden.shape
    rows = nmp * tokens
    deep = nz * half
    acts, width = query.shape
    others = max(nmp - 1, 1)
    bf16, f32 = jnp.bfloat16, jnp.float32
    order = stages(nz, chunks)
    return pl.pallas_call(
        functools.partial(kernel, order, nz, nmp, ratio),
        out_shape=(
            jax.ShapeDtypeStruct((acts, width), bf16),
            jax.ShapeDtypeStruct((acts, width), f32),
            jax.ShapeDtypeStruct(akv.shape, f32),
            jax.ShapeDtypeStruct((2 * half * chunks * 2, HD), f32),
        ),
        in_specs=[anywhere] * 3 + [smem] * 2 + [anywhere] * 5,
        out_specs=(vmem,) * 4,
        scratch_shapes=[
            pltpu.VMEM(gain.shape, f32),
            pltpu.VMEM((acts, rows + acts), f32),
            pltpu.VMEM(query.shape, bf16),
            pltpu.VMEM(akv.shape, bf16),
            pltpu.VMEM(cotangent.shape, bf16),
            pltpu.VMEM(pblocks.shape, jnp.int32),
            pltpu.VMEM(ablocks.shape, jnp.int32),
            pltpu.VMEM((half,) + weight.shape[1:], bf16),
            pltpu.VMEM((2, tokens // STRIPS, features), bf16),
            pltpu.VMEM((4, tokens, deep), bf16),
            pltpu.VMEM((chunks, half, PAIR), bf16),
            pltpu.VMEM((4, rows, deep), bf16),
            pltpu.VMEM((chunks, deep, PAIR), bf16),
            pltpu.VMEM((min(chunks, KEPT), 2, 2, rows // 2, PAIR), f32),
            pltpu.VMEM((chunks, 2, 2, rows // 2, PAIR), bf16),
            pltpu.VMEM((chunks, 2, 2, rows // 2, PAIR), bf16),
            pltpu.VMEM((chunks, 2, rows // 2, PAIR), bf16),
            pltpu.VMEM((chunks, 2, rows // 2, PAIR), bf16),
            pltpu.VMEM((chunks, 4, rows, PAIR), bf16),
            pltpu.VMEM((chunks, nz, half, PAIR), bf16),
            pltpu.VMEM((chunks, nz + 1, half, PAIR), bf16),
            dma((2, chunks, nz)), dma((chunks, nz)), dma((STRIPS,)), dma((1,)), dma((2,)), dma((6,)),
            dma((3, STRIPS)), dma((3, STRIPS)), dma((4, STRIPS, others)), dma((4, STRIPS, others)),
            dma((chunks, 2, 2)), dma((chunks, 2, 2)), dma((chunks, 2)), dma((chunks, 2)),
            dma((chunks, 3, 2)), dma((chunks, 3, 2)),
            dma((chunks, nz, CUTS)), dma((chunks, nz + 1, CUTS)),
            dma((chunks, CUTS)), dma((chunks, CUTS)),
        ],
        compiler_params=pltpu.CompilerParams(
            collective_id=0, has_side_effects=True, vmem_limit_bytes=int(LIMIT * MiB)
        ),
        name="fused",
    )(
        *[stay(a) for a in (weight, hidden, gain)],
        level,
        length,
        *[stay(a) for a in (query, akv, cotangent, pblocks, ablocks)],
    )


def settle_kernel(*refs):
    count = (len(refs) - 1) // 2
    copies = [
        pltpu.make_async_copy(src, dst, refs[-1].at[i])
        for i, (src, dst) in enumerate(zip(refs[:count], refs[count:-1]))
    ]
    for copy in copies:
        copy.start()
    for copy in copies:
        copy.wait()


def settle(*arrays):
    return pl.pallas_call(
        settle_kernel,
        out_shape=tuple(jax.ShapeDtypeStruct(a.shape, a.dtype) for a in arrays),
        in_specs=[pl.BlockSpec(memory_space=pl.ANY)] * len(arrays),
        out_specs=(pl.BlockSpec(memory_space=pltpu.HBM),) * len(arrays),
        scratch_shapes=[pltpu.SemaphoreType.DMA((len(arrays),))],
        compiler_params=pltpu.CompilerParams(vmem_limit_bytes=1 * MiB),
        name="settle",
    )(*arrays)


def shards(
    ndp,
    nmp,
    prefix_hidden,
    norm_gain,
    kv_weight,
    action_query,
    action_kv,
    out_cotangent,
    prefix_blocks,
    action_blocks,
    prefix_lengths,
    timesteps,
):
    nz = ndp // 2
    ratio = QH // KVH
    depth, _, columns = kv_weight.shape
    chunks = columns // HD
    level = 0.5 + (timesteps.astype(jnp.float32) + 0.5) / STEPS
    attn_out, query_grad, d_action, summed = fused(
        nz, nmp, ratio, kv_weight, prefix_hidden[0], norm_gain[None], level, prefix_lengths,
        action_query[0], action_kv[0], out_cotangent[0], prefix_blocks, action_blocks,
    )
    attn_out, query_grad, d_action, summed = settle(attn_out, query_grad, d_action, summed)
    weight_grad = summed.reshape(depth, chunks, 2, HD).transpose(0, 2, 1, 3).reshape(depth, 2, columns)
    return (
        attn_out[None],
        query_grad[None],
        d_action[None],
        weight_grad,
    )


def solution(mesh):
    placed = (
        P(("dp", "segment"), "mp", None),
        P(),
        P("dp", None, "mp"),
        P(("dp", "segment"), None, "mp"),
        P(("dp", "segment"), None, None, "mp"),
        P(("dp", "segment"), None, "mp"),
        P(("dp", "segment"), None),
        P(("dp", "segment"), None),
        P(("dp", "segment")),
        P(("dp", "segment")),
    )
    return jax.shard_map(
        functools.partial(shards, mesh.shape["dp"], mesh.shape["mp"]),
        mesh=mesh,
        in_specs=placed,
        out_specs=(
            P(("dp", "segment"), None, "mp"),
            P(("dp", "segment"), None, "mp"),
            P(("dp", "segment"), None, None, "mp"),
            P("dp", None, "mp"),
        ),
        check_vma=False,
    )
```

```python
import functools

import jax
import jax.numpy as jnp
from jax import lax
from jax.experimental import pallas as pl
from jax.experimental.pallas import tpu as pltpu
from jax.sharding import PartitionSpec as P

HD = 128
QH = 16
KVH = 8
STEPS = 1000
EPS = 1e-06
NEGATIVE = -1e30
MiB = 1 << 20
PAIR = 2 * HD
KEPT = 3
CUTS = 4
STRIPS = 8
LIMIT = 45.5


def remote(src, dst, send_sem, recv_sem, where):
    return pltpu.make_async_remote_copy(
        src_ref=src,
        dst_ref=dst,
        send_sem=send_sem,
        recv_sem=recv_sem,
        device_id=where,
        device_id_type=pl.DeviceIdType.MESH,
    )


class Plan:
    def __init__(self, nz, chunks):
        self.nz, self.chunks = nz, chunks
        self.free = dict(core=0.0, x=0.0, s=0.0, z=0.0, m=0.0)
        self.arrived = {}
        self.pending = []
        self.order = []

    def add(self, key, needs, cost, sends, rank):
        self.pending.append((key, needs, cost, sends, rank))

    def run(self):
        done = set()
        while self.pending:
            best = None
            for entry in self.pending:
                key, needs, cost, sends, rank = entry
                if any(n not in self.arrived for n in needs):
                    continue
                ready = max([self.free["core"]] + [self.arrived[n] for n in needs])
                pick = (ready, rank)
                if best is None or pick < best[0]:
                    best = (pick, entry)
            (ready, _), entry = best
            self.pending.remove(entry)
            key, needs, cost, sends, rank = entry
            self.order.append(key)
            self.arrived[key] = ready + cost
            self.free["core"] = ready + cost
            for name, link, size in sends:
                start = max(ready + cost, self.free[link])
                self.free[link] = start + size
                self.arrived[name] = start + size + HOP
        return self.order


UNIT = 5.7
HOP = 1.7


FOUND = (
    ("ns", 0), ("wo", 0), ("ns", 1), ("ns", 2), ("ns", 3), ("ns", 4), ("ns", 5), ("wo", 1),
    ("wf", 0, 1), ("wf", 1, 1), ("wo", 2), ("wo", 3), ("ns", 6), ("ns", 7), ("wf", 2, 1), ("nf", 0),
    ("nf", 1), ("nf", 2), ("nf", 3), ("wf", 0, 2), ("nf", 4), ("nf", 5), ("wf", 1, 2), ("wf", 2, 2),
    ("nf", 6), ("nf", 7), ("wf", 0, 3), ("A", 0), ("B", 0, 1), ("wf", 1, 3), ("wf", 3, 1), ("B", 0, 0),
    ("A", 1), ("C", 0), ("wf", 2, 3), ("G", 0, 0), ("G", 0, 1), ("B", 1, 1), ("B", 1, 0), ("wf", 3, 2),
    ("A", 2), ("E", 0, 3), ("C", 1), ("E", 0, 2), ("G", 1, 1), ("E", 0, 1), ("G", 1, 0), ("B", 2, 1),
    ("wf", 3, 3), ("B", 2, 0), ("A", 3), ("E", 1, 3), ("E", 1, 2), ("C", 2), ("E", 1, 1), ("G", 2, 1),
    ("G", 2, 0), ("B", 3, 0), ("F", 0), ("B", 3, 1), ("E", 2, 3), ("E", 2, 2), ("C", 3), ("H", 0),
    ("E", 2, 1), ("G", 3, 0), ("G", 3, 1), ("F", 1), ("E", 3, 3), ("F", 2), ("E", 3, 2), ("H", 1),
    ("E", 3, 1), ("H", 2), ("F", 3), ("H", 3),
)


def stages(nz, chunks):
    made = modelled(nz, chunks)
    return list(FOUND) if set(FOUND) == set(made) else made


def modelled(nz, chunks):
    plan = Plan(nz, chunks)
    piece = UNIT
    for c in range(chunks):
        needs = [] if c < 2 else [("wf", c - 2, nz - 1)]
        plan.add(("wo", c), needs, 0.1, [(("w", c, 1), "z", piece)], c * 0.01)
        for k in range(1, nz):
            needs = [("w", c, k)] + ([("wf", c, k - 1)] if k > 1 else [("wo", c)])
            sends = [(("w", c, k + 1), "z", piece)] if k < nz - 1 else []
            plan.add(("wf", c, k), needs, 0.1, sends, 1)
    for j in range(STRIPS):
        needs = [("ns", j - 1)] if j else [("wo", 0)]
        plan.add(
            ("ns", j), needs, 0.1,
            [(("nx", j), "x", piece), (("ny", j), "s", piece), (("nd", j), "x", piece), (("nd2", j), "s", piece)], 0.005,
        )
        plan.add(("nf", j), [("nx", j), ("ny", j), ("nd", j), ("nd2", j)], 0.1, [(("nm", j), "m", 2.0)], 2)
    for c in range(chunks):
        needs = [("nm", j) for j in range(STRIPS)] + [("wf", c, k) for k in range(1, nz)]
        if c >= KEPT:
            needs.append(("C", c - KEPT))
        plan.add(("A", c), needs, 3.0, [(("p0", c), "x", piece), (("p1", c), "s", piece)], 10 + c)
        plan.add(("B", c, 0), [("A", c), ("p0", c)], 0.3, [(("y0", c), "s", piece / 2)], 7)
        plan.add(("B", c, 1), [("A", c), ("p1", c)], 0.3, [(("y1", c), "x", piece / 2)], 7)
        plan.add(
            ("C", c), [("B", c, 0), ("B", c, 1), ("y0", c), ("y1", c)], 2.5,
            [
                (("gx1", c), "x", piece / 2), (("gs0", c), "s", piece / 2),
                (("gx0", c), "x", piece / 2), (("gs1", c), "s", piece / 2),
            ], 6,
        )
        plan.add(("G", c, 0), [("C", c), ("gs0", c)], 0.1, [(("gf0", c), "x", piece / 2)], 4)
        plan.add(("G", c, 1), [("C", c), ("gx1", c)], 0.1, [(("gf1", c), "s", piece / 2)], 4)
        full = [("G", c, 0), ("G", c, 1), ("gx0", c), ("gs1", c), ("gf0", c), ("gf1", c)]
        for off in range(nz - 1, 0, -1):
            needs = full if off == nz - 1 else [("E", c, off + 1), ("e", c, off + 1)]
            plan.add(("E", c, off), needs, 1.2, [(("e", c, off), "z", piece)], 3)
        plan.add(("F", c), [("E", c, 1), ("e", c, 1)], 1.3, [(("o", c), "s", piece)], 5)
        plan.add(("H", c), [("F", c), ("o", c)], 0.5, [], 20)
    return plan.run()


def kernel(
    order, nz, nmp, ratio,
    w_hbm, h_hbm, gain_hbm, level_ref, length_ref, q_hbm, akv_hbm, cot_hbm, pb_hbm, ab_hbm,
    out_ref, dq_ref, dakv_ref, grad_ref,
    gain_ref, vis_ref, q_ref, akv_ref, cot_ref, pb_ref, ab_ref, w_raw, h_buf, n_ref, o_ref, nb, wb, keep, ps, px, ys, yb, gb, zs, zb,
    w_send, w_recv, own_n, load_w, load_h, load_more, n_send, n_recv, f_send, f_recv,
    p_send, p_recv, y_send, y_recv, g_send, g_recv, z_send, z_recv, o_send, o_recv,
):
    dp, seg, mp = lax.axis_index("dp"), lax.axis_index("segment"), lax.axis_index("mp")
    z, x = dp // 2, dp % 2
    chunks, half = wb.shape[0], w_raw.shape[0]
    tokens, features = h_hbm.shape
    strip = tokens // STRIPS
    samples, rows = nb.shape[0], nb.shape[1]
    others = nmp - 1
    acts = q_ref.shape[0]
    scale = HD ** (-0.5)

    x_dp = z * 2 + (1 - x)
    plane = [
        {"dp": x_dp},
        {"segment": 1 - seg},
        {"dp": x_dp, "segment": 1 - seg},
    ]
    plane_xs = [(1 - x, seg), (x, 1 - seg), (1 - x, 1 - seg)]
    m_peer = [{"mp": (mp + o) % nmp} for o in range(1, nmp)]
    up = {"dp": (z + 1) * 2 + x}
    down = {"dp": (z - 1) * 2 + x}
    has_up, has_down = z < nz - 1, z > 0
    mine = x * 2 + seg

    def h_load(j):
        return pltpu.make_async_copy(h_hbm.at[pl.ds(j * strip, strip)], h_buf.at[j % 2], load_h.at[j % 2])

    w_load = pltpu.make_async_copy(w_hbm.at[pl.ds(pl.multiple_of(seg * half, half), half)], w_raw, load_w.at[0])
    more = [
        pltpu.make_async_copy(src, dst, load_more.at[i])
        for i, (src, dst) in enumerate(
            [(gain_hbm, gain_ref), (q_hbm, q_ref), (akv_hbm, akv_ref), (cot_hbm, cot_ref), (pb_hbm, pb_ref), (ab_hbm, ab_ref)]
        )
    ]
    h_load(0).start()
    more[0].start()
    w_load.start()
    h_load(1).start()
    for copy in more[1:]:
        copy.start()

    barrier = pltpu.get_barrier_semaphore()
    for peer in plane + m_peer:
        pl.semaphore_signal(barrier, inc=1, device_id=peer, device_id_type=pl.DeviceIdType.MESH)

    @pl.when(has_up)
    def _():
        pl.semaphore_signal(barrier, inc=1, device_id=up, device_id_type=pl.DeviceIdType.MESH)

    @pl.when(has_down)
    def _():
        pl.semaphore_signal(barrier, inc=1, device_id=down, device_id_type=pl.DeviceIdType.MESH)

    ends = has_up.astype(jnp.int32) + has_down.astype(jnp.int32)
    pl.semaphore_wait(barrier, len(plane) + len(m_peer) + ends)

    def block(b):
        return pl.ds(pl.multiple_of(b * half, half), half)

    def rows_of(m, j):
        return pl.ds(pl.multiple_of(m * tokens + j * strip, strip), strip)

    def dot(a, b, ca, cb):
        return lax.dot_general(a, b, (((ca,), (cb,)), ((), ())), preferred_element_type=jnp.float32)

    def w_copy(c, k, upward):
        src_block = z - k if upward else z + k
        part = wb.at[c, block(src_block)]
        return remote(
            part, part,
            w_send.at[int(upward), c, k], w_recv.at[c, src_block], up if upward else down,
        )

    def w_arrival(c, k, upward):
        src_block = z - k if upward else z + k
        part = wb.at[c, block(src_block)]
        return remote(part, part, w_send.at[int(upward), c, k], w_recv.at[c, src_block], down if upward else up)

    def weights_own(c):
        if c == 0:
            w_load.wait()
        group = min(half, 128)

        @pl.loop(0, half // group)
        def _(i):
            first = pl.multiple_of(i * group, group)
            for kv in range(2):
                wb[c, pl.ds(pl.multiple_of(z * half + first, group), group), kv * HD : (kv + 1) * HD] = w_raw[
                    pl.ds(first, group), kv, c * HD : (c + 1) * HD
                ]

        @pl.when(has_up)
        def _():
            w_copy(c, 0, True).start()

        @pl.when(has_down)
        def _():
            w_copy(c, 0, False).start()

    def weights_forward(c, k):
        @pl.when(z - k >= 0)
        def _():
            w_arrival(c, k, True).wait_recv()
            if k < nz - 1:
                @pl.when(has_up)
                def _():
                    w_copy(c, k, True).start()

        @pl.when(z + k < nz)
        def _():
            w_arrival(c, k, False).wait_recv()
            if k < nz - 1:
                @pl.when(has_down)
                def _():
                    w_copy(c, k, False).start()

    plane_q = [a * 2 + b for a, b in plane_xs]

    def n_copy(p, j):
        return remote(
            n_ref.at[plane_q[p], pl.ds(j * strip, strip)], nb.at[mine, rows_of(mp, j)],
            n_send.at[p, j], n_recv.at[p, j], plane[p],
        )

    def n_keep(j):
        return pltpu.make_async_copy(
            n_ref.at[mine, pl.ds(j * strip, strip)], nb.at[mine, rows_of(mp, j)], own_n.at[j]
        )

    def f_copy(p, j, o):
        if p == 3:
            return remote(
                n_ref.at[mine, pl.ds(j * strip, strip)], nb.at[mine, rows_of(mp, j)],
                f_send.at[p, j, o], f_recv.at[p, j, o], m_peer[o],
            )
        part = nb.at[plane_q[p], rows_of(mp, j)]
        return remote(part, part, f_send.at[p, j, o], f_recv.at[p, j, o], m_peer[o])

    def normalize(j):
        h_load(j).wait()
        if j == 0:
            more[0].wait()
        group = min(strip, 16)
        wide = 1024 if features % 1024 == 0 else half

        @pl.loop(0, strip // group)
        def _(i):
            part = pl.ds(pl.multiple_of(i * group, group), group)
            into = pl.ds(pl.multiple_of(j * strip + i * group, group), group)
            total = jnp.zeros((group, 1), jnp.float32)
            for k in range(0, features, wide):
                piece = h_buf[j % 2, part, k : k + wide].astype(jnp.float32)
                total = total + jnp.sum(piece * piece, axis=-1, keepdims=True)
            inverse = lax.rsqrt(total / features + EPS)
            for b in range(nz):
                for q in range(4):
                    first = (b * 4 + q) * half
                    piece = h_buf[j % 2, part, first : first + half].astype(jnp.float32)
                    scaled = piece * inverse * gain_ref[:, first : first + half]
                    n_ref[q, into, b * half : (b + 1) * half] = scaled.astype(jnp.bfloat16)

        if j + 2 < STRIPS:
            h_load(j + 2).start()

    def tokens_send(j):
        normalize(j)
        for p in (2, 0, 1):
            n_copy(p, j).start()
        n_keep(j).start()
        for o in range(others):
            f_copy(3, j, o).start()

    def tokens_forward(j):
        for p in range(3):
            n_copy(p, j).wait_recv()
            for o in range(others):
                f_copy(p, j, o).start()

    def tokens_wait():
        for j in range(STRIPS):
            n_keep(j).wait()
            for p in range(4):
                for o in range(others):
                    f_copy(p, j, o).wait_recv()

    part_rows = rows // 2
    halves = [pl.ds(0, part_rows), pl.ds(part_rows, part_rows)]
    spot = [seg, x]

    def sample(h, first, second):
        return first * 2 + second if h == 0 else second * 2 + first

    def p_copy(c, h, i):
        b = spot[h] if i else 1 - spot[h]
        return remote(ps.at[c, h, b], px.at[c, h, b], p_send.at[c, h, i], p_recv.at[c, h, i], plane[h])

    def y_copy(c, h):
        return remote(ys.at[c, h], yb.at[c, h], y_send.at[c, h], y_recv.at[c, h], plane[1 - h])

    def partial_sums(c):
        if c == 0:
            tokens_wait()
        for i in range(2):
            for h in range(2):
                b = spot[h] if i else 1 - spot[h]
                q = sample(h, 1 - (x, seg)[h], b)
                ps[c, h, b] = dot(nb[q, halves[h], :], wb[c], 1, 0).astype(jnp.bfloat16)
                p_copy(c, h, i).start()
        for h in range(2):
            @pl.loop(0, 2)
            def _(b):
                q = sample(h, (x, seg)[h], b)
                keep[c % KEPT, h, b] = dot(nb[q, halves[h], :], wb[c], 1, 0)

    def second_sums(c, h):
        b = spot[h]
        p_copy(c, h, 0).wait_recv()
        ys[c, h] = (keep[c % KEPT, h, 1 - b] + px[c, h, 1 - b].astype(jnp.float32)).astype(jnp.bfloat16)
        y_copy(c, h).start()

    def g_copy(c, to, h):
        part = gb.at[c, mine, halves[h]]
        return remote(part, part, g_send.at[c, to, h], g_recv.at[c, to, h], plane[to])

    def g_forward(c, h):
        q = sample(h, (x, seg)[h], 1 - spot[h])
        part = gb.at[c, q, halves[h]]
        return remote(part, part, g_send.at[c, 2, h], g_recv.at[c, 2, h], plane[h])

    def visible_tokens():
        wide = jnp.broadcast_to(ab_ref[...].astype(jnp.float32), (acts, acts))
        levels = wide.T
        see_action = wide <= levels
        levels = jnp.concatenate([levels] * (rows // acts), axis=1)
        place = lax.broadcasted_iota(jnp.int32, (acts, rows), 1)
        see_prefix = (pb_ref[...].astype(jnp.float32) <= levels) & (place < length_ref[0])
        return jnp.concatenate([see_prefix.astype(jnp.float32), see_action.astype(jnp.float32)], axis=1)

    def attend(c):
        if c == 0:
            for copy in more[1:]:
                copy.wait()
            vis_ref[...] = visible_tokens()
        visible = jnp.concatenate([vis_ref[...]] * ratio, axis=0) > 0.5
        parts = []
        for h in range(2):
            y_copy(c, h).wait_recv()
            p_copy(c, h, 1).wait_recv()
            b = spot[h]
            parts.append(
                keep[c % KEPT, h, b] + px[c, h, b].astype(jnp.float32) + yb[c, h].astype(jnp.float32)
            )
        pair = jnp.concatenate(parts, axis=0).astype(jnp.bfloat16)
        cols = slice(c * HD, (c + 1) * HD)
        keys = jnp.concatenate([pair[:, :HD], akv_ref[:, 0, cols]], axis=0)
        values = jnp.concatenate([pair[:, HD:], akv_ref[:, 1, cols]], axis=0)
        hs = [slice((c * ratio + r) * HD, (c * ratio + r + 1) * HD) for r in range(ratio)]
        query = jnp.concatenate([q_ref[:, h] for h in hs], axis=0)
        cot = jnp.concatenate([cot_ref[:, h] for h in hs], axis=0)
        go = (level_ref[0] * cot.astype(jnp.float32)).astype(jnp.bfloat16)
        masked = jnp.where(visible, dot(query, keys, 1, 1) * scale, NEGATIVE)
        top = jnp.max(masked, axis=-1, keepdims=True)
        expo = jnp.where(visible, jnp.exp(masked - top), 0.0)
        probs = expo * (1.0 / jnp.sum(expo, axis=-1, keepdims=True))
        low = probs.astype(jnp.bfloat16)
        d_probs = dot(go, values, 1, 1)
        delta = jnp.sum(probs * d_probs, axis=-1, keepdims=True)
        d_scores = (probs * (d_probs - delta)).astype(jnp.bfloat16)
        d_keys = dot(d_scores, query, 0, 0) * scale
        d_values = dot(low, go, 0, 0)
        gb[c, mine, :, :HD] = d_keys[:rows].astype(jnp.bfloat16)
        gb[c, mine, :, HD:] = d_values[:rows].astype(jnp.bfloat16)
        for h in range(2):
            g_copy(c, 0, 1 - h).start()
            g_copy(c, 1, h).start()
        dakv_ref[:, 0, cols] = d_keys[rows:]
        dakv_ref[:, 1, cols] = d_values[rows:]
        out = dot(low, values, 1, 0).astype(jnp.bfloat16)
        d_query = dot(d_scores, keys, 1, 0) * scale
        for r, h in enumerate(hs):
            out_ref[:, h] = out[r * acts : (r + 1) * acts]
            dq_ref[:, h] = d_query[r * acts : (r + 1) * acts]

    def grads_forward(c, h):
        g_copy(c, 1 - h, h).wait_recv()
        g_forward(c, h).start()

    def grads_wait(c):
        for h in range(2):
            g_copy(c, h, h).wait_recv()
            g_forward(c, h).wait_recv()

    cuts = next(n for n in (CUTS, 2, 1) if half % (n * 128) == 0)
    depth = half // cuts

    def weight_term(c, b, i):
        cols = pl.ds(pl.multiple_of(b * half + i * depth, depth), depth)
        total = dot(nb[0, :, cols], gb[c, 0], 0, 0)
        for q in range(1, samples):
            total = total + dot(nb[q, :, cols], gb[c, q], 0, 0)
        return total

    def half_of(i):
        return pl.ds(pl.multiple_of(i * depth, depth), depth)

    def z_copy(c, off, upward, i):
        to = z + off if upward else z - off
        slot = nz if (not upward and off == 1) else to
        return remote(
            zs.at[c, to, half_of(i)], zb.at[c, slot, half_of(i)],
            z_send.at[c, to, i], z_recv.at[c, slot, i], up if upward else down,
        )

    def z_arrival(c, slot, upward, i):
        part = zb.at[c, slot, half_of(i)]
        return remote(part, part, z_send.at[c, z, i], z_recv.at[c, slot, i], down if upward else up)

    def chain(c, off):
        if off == nz - 1:
            grads_wait(c)

        def step(to, upward):
            @pl.loop(0, cuts)
            def _(i):
                total = weight_term(c, to, i)

                @pl.when(has_down if upward else has_up)
                def _():
                    z_arrival(c, to, upward, i).wait_recv()

                zs[c, to, half_of(i), :] = (total + zb[c, to, half_of(i), :].astype(jnp.float32)).astype(jnp.bfloat16)
                z_copy(c, off, upward, i).start()

        @pl.when(z + off < nz)
        def _():
            step(z + off, True)

        @pl.when(z - off >= 0)
        def _():
            step(z - off, False)

    def o_copy(c, i):
        return remote(
            zs.at[c, z, half_of(i)], o_ref.at[c, half_of(i)], o_send.at[c, i], o_recv.at[c, i], plane[1]
        )

    def finish(c):
        @pl.loop(0, cuts)
        def _(i):
            part = half_of(i)
            total = weight_term(c, z, i)

            @pl.when(has_down)
            def _():
                z_arrival(c, z, True, i).wait_recv()

            @pl.when(has_up)
            def _():
                z_arrival(c, nz, False, i).wait_recv()

            total = total + zb[c, z, part, :].astype(jnp.float32) + zb[c, nz, part, :].astype(jnp.float32)
            zs[c, z, part, :] = total.astype(jnp.bfloat16)
            o_copy(c, i).start()

        spread(c, seg, zs.at[c, z])

    def spread(c, which, src):
        for i in range(2):
            first = which * (half * 2 * chunks) + c * 2 + i
            part = pl.ds(first, half, stride=2 * chunks)
            grad_ref[part, :] = src[:, i * HD : (i + 1) * HD].astype(jnp.float32)

    def other_half(c):
        for i in range(cuts):
            o_copy(c, i).wait()
            for kv in range(2):
                first = ((1 - seg) * half + i * depth) * (2 * chunks) + c * 2 + kv
                part = pl.ds(first, depth, stride=2 * chunks)
                grad_ref[part, :] = o_ref[c, i * depth : (i + 1) * depth, kv * HD : (kv + 1) * HD].astype(jnp.float32)

    def clear():
        @pl.when(z == 0)
        def _():
            @pl.loop(0, chunks)
            def _(c):
                @pl.loop(0, nz)
                def _(b):
                    zb[c, b] = jnp.zeros(zb.shape[2:], zb.dtype)

        @pl.when(z == nz - 1)
        def _():
            @pl.loop(0, chunks)
            def _(c):
                @pl.loop(0, nz - 1)
                def _(b):
                    zb[c, b] = jnp.zeros(zb.shape[2:], zb.dtype)

                zb[c, nz] = jnp.zeros(zb.shape[2:], zb.dtype)

    bodies = dict(
        wo=weights_own, wf=weights_forward, ns=tokens_send, nf=tokens_forward,
        A=partial_sums, B=second_sums, C=attend, G=grads_forward, E=chain, F=finish, H=other_half,
    )
    cleared = False
    for stage in order:
        if stage[0] not in ("wo", "ns") and not cleared:
            clear()
            cleared = True
        bodies[stage[0]](*stage[1:])

    for c in range(chunks):
        for h in range(2):
            p_copy(c, h, 0).wait_send()
            p_copy(c, h, 1).wait_send()
            y_copy(c, h).wait_send()
            for to in range(2):
                g_copy(c, to, h).wait_send()
            g_forward(c, h).wait_send()
        for off in range(nz - 1, 0, -1):
            @pl.when(z + off < nz)
            def _():
                for i in range(cuts):
                    z_copy(c, off, True, i).wait_send()

            @pl.when(z - off >= 0)
            def _():
                for i in range(cuts):
                    z_copy(c, off, False, i).wait_send()

        for k in range(nz - 1):
            @pl.when(jnp.logical_and(has_up, z - k >= 0))
            def _():
                w_copy(c, k, True).wait_send()

            @pl.when(jnp.logical_and(has_down, z + k < nz))
            def _():
                w_copy(c, k, False).wait_send()

    for j in range(STRIPS):
        for p in range(3):
            n_copy(p, j).wait_send()
        for p in range(4):
            for o in range(others):
                f_copy(p, j, o).wait_send()


def stay(array):
    return pltpu.with_memory_space_constraint(array, pltpu.HBM)


def fused(nz, nmp, ratio, weight, hidden, gain, level, length, query, akv, cotangent, pblocks, ablocks):
    dma = pltpu.SemaphoreType.DMA
    vmem = pl.BlockSpec(memory_space=pltpu.VMEM)
    smem = pl.BlockSpec(memory_space=pltpu.SMEM)
    anywhere = pl.BlockSpec(memory_space=pltpu.HBM)
    half, chunks = weight.shape[0] // 2, weight.shape[2] // HD
    tokens, features = hidden.shape
    rows = nmp * tokens
    deep = nz * half
    acts, width = query.shape
    others = max(nmp - 1, 1)
    bf16, f32 = jnp.bfloat16, jnp.float32
    order = stages(nz, chunks)
    return pl.pallas_call(
        functools.partial(kernel, order, nz, nmp, ratio),
        out_shape=(
            jax.ShapeDtypeStruct((acts, width), bf16),
            jax.ShapeDtypeStruct((acts, width), f32),
            jax.ShapeDtypeStruct(akv.shape, f32),
            jax.ShapeDtypeStruct((2 * half * chunks * 2, HD), f32),
        ),
        in_specs=[anywhere] * 3 + [smem] * 2 + [anywhere] * 5,
        out_specs=(vmem,) * 4,
        scratch_shapes=[
            pltpu.VMEM(gain.shape, f32),
            pltpu.VMEM((acts, rows + acts), f32),
            pltpu.VMEM(query.shape, bf16),
            pltpu.VMEM(akv.shape, bf16),
            pltpu.VMEM(cotangent.shape, bf16),
            pltpu.VMEM(pblocks.shape, jnp.int32),
            pltpu.VMEM(ablocks.shape, jnp.int32),
            pltpu.VMEM((half,) + weight.shape[1:], bf16),
            pltpu.VMEM((2, tokens // STRIPS, features), bf16),
            pltpu.VMEM((4, tokens, deep), bf16),
            pltpu.VMEM((chunks, half, PAIR), bf16),
            pltpu.VMEM((4, rows, deep), bf16),
            pltpu.VMEM((chunks, deep, PAIR), bf16),
            pltpu.VMEM((min(chunks, KEPT), 2, 2, rows // 2, PAIR), f32),
            pltpu.VMEM((chunks, 2, 2, rows // 2, PAIR), bf16),
            pltpu.VMEM((chunks, 2, 2, rows // 2, PAIR), bf16),
            pltpu.VMEM((chunks, 2, rows // 2, PAIR), bf16),
            pltpu.VMEM((chunks, 2, rows // 2, PAIR), bf16),
            pltpu.VMEM((chunks, 4, rows, PAIR), bf16),
            pltpu.VMEM((chunks, nz, half, PAIR), bf16),
            pltpu.VMEM((chunks, nz + 1, half, PAIR), bf16),
            dma((2, chunks, nz)), dma((chunks, nz)), dma((STRIPS,)), dma((1,)), dma((2,)), dma((6,)),
            dma((3, STRIPS)), dma((3, STRIPS)), dma((4, STRIPS, others)), dma((4, STRIPS, others)),
            dma((chunks, 2, 2)), dma((chunks, 2, 2)), dma((chunks, 2)), dma((chunks, 2)),
            dma((chunks, 3, 2)), dma((chunks, 3, 2)),
            dma((chunks, nz, CUTS)), dma((chunks, nz + 1, CUTS)),
            dma((chunks, CUTS)), dma((chunks, CUTS)),
        ],
        compiler_params=pltpu.CompilerParams(
            collective_id=0, has_side_effects=True, vmem_limit_bytes=int(LIMIT * MiB)
        ),
        name="fused",
    )(
        *[stay(a) for a in (weight, hidden, gain)],
        level,
        length,
        *[stay(a) for a in (query, akv, cotangent, pblocks, ablocks)],
    )


def settle_kernel(*refs):
    count = (len(refs) - 1) // 2
    copies = [
        pltpu.make_async_copy(src, dst, refs[-1].at[i])
        for i, (src, dst) in enumerate(zip(refs[:count], refs[count:-1]))
    ]
    for copy in copies:
        copy.start()
    for copy in copies:
        copy.wait()


def settle(*arrays):
    return pl.pallas_call(
        settle_kernel,
        out_shape=tuple(jax.ShapeDtypeStruct(a.shape, a.dtype) for a in arrays),
        in_specs=[pl.BlockSpec(memory_space=pl.ANY)] * len(arrays),
        out_specs=(pl.BlockSpec(memory_space=pltpu.HBM),) * len(arrays),
        scratch_shapes=[pltpu.SemaphoreType.DMA((len(arrays),))],
        compiler_params=pltpu.CompilerParams(vmem_limit_bytes=1 * MiB),
        name="settle",
    )(*arrays)


def shards(
    ndp,
    nmp,
    prefix_hidden,
    norm_gain,
    kv_weight,
    action_query,
    action_kv,
    out_cotangent,
    prefix_blocks,
    action_blocks,
    prefix_lengths,
    timesteps,
):
    nz = ndp // 2
    ratio = QH // KVH
    depth, _, columns = kv_weight.shape
    chunks = columns // HD
    level = 0.5 + (timesteps.astype(jnp.float32) + 0.5) / STEPS
    attn_out, query_grad, d_action, summed = fused(
        nz, nmp, ratio, kv_weight, prefix_hidden[0], norm_gain[None], level, prefix_lengths,
        action_query[0], action_kv[0], out_cotangent[0], prefix_blocks, action_blocks,
    )
    attn_out, query_grad, d_action, summed = settle(attn_out, query_grad, d_action, summed)
    weight_grad = summed.reshape(depth, chunks, 2, HD).transpose(0, 2, 1, 3).reshape(depth, 2, columns)
    return (
        attn_out[None],
        query_grad[None],
        d_action[None],
        weight_grad,
    )


def solution(mesh):
    placed = (
        P(("dp", "segment"), "mp", None),
        P(),
        P("dp", None, "mp"),
        P(("dp", "segment"), None, "mp"),
        P(("dp", "segment"), None, None, "mp"),
        P(("dp", "segment"), None, "mp"),
        P(("dp", "segment"), None),
        P(("dp", "segment"), None),
        P(("dp", "segment")),
        P(("dp", "segment")),
    )
    return jax.shard_map(
        functools.partial(shards, mesh.shape["dp"], mesh.shape["mp"]),
        mesh=mesh,
        in_specs=placed,
        out_specs=(
            P(("dp", "segment"), None, "mp"),
            P(("dp", "segment"), None, "mp"),
            P(("dp", "segment"), None, None, "mp"),
            P("dp", None, "mp"),
        ),
        check_vma=False,
    )
```
